32 devices in a mesh: inst: 8 (over z, y), space: 4 (over x, core).
Axes of the slice: x: 2, y: 2, z: 4, core: 2. Of those that a mesh axis runs over, the one named last changes fastest.
Arguments:
- state: float32 [32, 320, 512], P('inst', None, 'space'), may hold values from -6 to 6
- forcing: float32 [32, 320, 512], P('inst', None, 'space'), may hold values from -6 to 6
- flux_jac: float32 [3, 5, 5], replicated, may hold values from -0.875 to 0.875
- jacobi_inv: float32 [32, 320, 320], P('inst'), may hold values from -0.01 to 0.03
- cross_nbr: int32 [4, 64], replicated, may hold values from 0 to 63, as said below
- lower_match: int32 [32, 4, 64], P('inst', 'space'), may hold values from 0 to 63, as said below
Outputs:
- residual: float32 [32, 320, 512], P('inst', None, 'space')
- updated: float32 [32, 320, 512], P('inst', None, 'space')
The draws below stay inside these ranges and needn't reach their ends.
Inputs may be any that keep to these rules, and one draw needn't show every extreme that they name: `cross_nbr`: the cells form a grid of 8 by 8, periodic in both directions, in an order drawn from the seed; if row 0 names n for cell c then row 1 names c for n, and likewise rows 2 and 3. lower_match[t, p] is the identity except at the sliding interface p = 4 // 2, where it is the cyclic pitch shift of the cross_nbr grid by (t * 8 // 32 + r) % 8 rows, with one offset r drawn from the seed: the cell below that faces c is the one reached from c by that many steps through row 1 of cross_nbr.
All inputs are finite; a program needn't handle non-finite values.
Results may differ from the reference program's by a relative error of at most 0.0003.
Values sent between devices are 32-bit elements; how exact they have to be, the bound alone decides.
A program may use at most 128 MiB of HBM per device.

```python
import math
import jax
import jax.numpy as jnp
import numpy as np
from jax import lax

TIME_INSTANCES = 32
VARS = 5
NODE1 = 4
BLOCK = 320
EX = 2
PITCH_ELEMENTS = 8
EZ = 8
ELEMENTS = 512
SWEEPS = 2
N_SPACE = 4


def draw_jacobi_inv(key, part):
    noise = jnp.clip(jax.random.normal(key, (TIME_INSTANCES, BLOCK, BLOCK), jnp.float32), -4.0, 4.0)
    eye = jnp.eye(BLOCK, dtype=jnp.float32)
    base = 0.015 * eye[None] + 0.012 * noise / jnp.sqrt(jnp.float32(BLOCK))
    return base


def grid_order(key):
    cells = PITCH_ELEMENTS * EZ
    place = jax.random.permutation(jax.random.fold_in(key, 3), cells).astype(jnp.int32)
    owner = jnp.argsort(place).astype(jnp.int32)
    return (place, owner)


def draw_cross_nbr(key, part):
    place, owner = grid_order(key)
    row_pos = place // EZ
    col_pos = place % EZ
    minus_pitch = owner[(row_pos - 1) % PITCH_ELEMENTS * EZ + col_pos]
    plus_pitch = owner[(row_pos + 1) % PITCH_ELEMENTS * EZ + col_pos]
    minus_span = owner[row_pos * EZ + (col_pos - 1) % EZ]
    plus_span = owner[row_pos * EZ + (col_pos + 1) % EZ]
    return jnp.stack([minus_pitch, plus_pitch, minus_span, plus_span]).astype(jnp.int32)


def draw_lower_match(key, part):
    cells = PITCH_ELEMENTS * EZ
    place, owner = grid_order(key)
    row_pos = place // EZ
    col_pos = place % EZ
    pitch_offset = jax.random.randint(jax.random.fold_in(key, 11), (), 0, PITCH_ELEMENTS).astype(jnp.int32)
    period_samples = jnp.arange(TIME_INSTANCES, dtype=jnp.int32)
    phase_shifts = (period_samples * PITCH_ELEMENTS // TIME_INSTANCES + pitch_offset) % PITCH_ELEMENTS
    shifted = owner[(row_pos[None, :] + phase_shifts[:, None]) % PITCH_ELEMENTS * EZ + col_pos[None, :]].astype(jnp.int32)
    identity_map = jnp.broadcast_to(jnp.arange(cells, dtype=jnp.int32)[None, None, :], (TIME_INSTANCES, N_SPACE, cells))
    sliding = (jnp.arange(N_SPACE, dtype=jnp.int32) == N_SPACE // 2)[None, :, None]
    return jnp.where(sliding, shifted[:, None, :], identity_map).astype(jnp.int32)


def level_of(own_key, extent, cuts, low, top_value):
    factor_of, own = 1.0, jax.random.fold_in(own_key, 6)
    for position, shards_of in cuts:
        heights = jnp.exp(jax.random.uniform(jax.random.fold_in(own, position), (shards_of,), jnp.float32, low / len(cuts), top_value / len(cuts)))
        factor_of = factor_of * jnp.repeat(heights, extent[position] // shards_of).reshape([-1 if axis == position else 1 for axis in range(len(extent))])
    return factor_of


def bell_draw(stream_key, extent, scale, most, cuts=(), kind=jnp.bfloat16):
    drawn = scale * jax.random.normal(stream_key, extent, jnp.float32)
    if cuts:
        drawn = drawn * level_of(stream_key, extent, cuts, -0.22, 0.18)
    return jnp.clip(drawn, -most, most).astype(kind)


def setup_inputs(seed: int = 0) -> dict:
    keys = jax.random.split(jax.random.key(seed), 7)
    return {
        "state": bell_draw(keys[0], (TIME_INSTANCES, BLOCK, ELEMENTS), 1.0, 6.0, ((0, 8), (2, 4)), jnp.float32),
        "forcing": bell_draw(keys[1], (TIME_INSTANCES, BLOCK, ELEMENTS), 1.0, 6.0, ((0, 8), (2, 4)), jnp.float32),
        "flux_jac": bell_draw(keys[2], (3, VARS, VARS), (9 * VARS) ** -0.5, 0.875, (), jnp.float32),
        "jacobi_inv": draw_jacobi_inv(jax.random.fold_in(keys[6], 71), 0),
        "cross_nbr": draw_cross_nbr(jax.random.fold_in(keys[6], 71), 0),
        "lower_match": draw_lower_match(jax.random.fold_in(keys[6], 71), 0),
    }


dissipation = 0.6
frequency = 0.25

def lobatto_derivative(count_of_nodes):
    inner_point = math.sqrt(0.2)
    points = np.array([-1.0, -inner_point, inner_point, 1.0])
    barycentric = np.ones(count_of_nodes)
    for first_index in range(count_of_nodes):
        for second_index in range(count_of_nodes):
            if first_index != second_index:
                barycentric[first_index] = barycentric[first_index] / (points[first_index] - points[second_index])
    table = np.zeros((count_of_nodes, count_of_nodes))
    for first_index in range(count_of_nodes):
        for second_index in range(count_of_nodes):
            if first_index != second_index:
                table[first_index, second_index] = barycentric[second_index] / barycentric[first_index] / (points[first_index] - points[second_index])
        table[first_index, first_index] = -np.sum(table[first_index])
    return table

def surface_term(plus, minus, jacobian, sign):
    matrix = sign * jacobian - dissipation * jnp.eye(jacobian.shape[0], dtype=jnp.float32)
    return jnp.einsum('wv,vabg->wabg', matrix, plus - minus, precision=lax.Precision.HIGHEST)

def spatial_residual(field, flux_jac, derivative, cross_nbr, match):
    nodes = derivative.shape[0]
    width = flux_jac.shape[1]
    cells = cross_nbr.shape[1]
    total = field.shape[1]
    layers = total // cells
    highest = lax.Precision.HIGHEST
    reshaped_array = field.reshape(width, nodes, nodes, nodes, total)
    along_x = jnp.einsum('ai,vijkg->vajkg', derivative, reshaped_array, precision=highest)
    along_y = jnp.einsum('aj,vijkg->viakg', derivative, reshaped_array, precision=highest)
    along_z = jnp.einsum('ak,vijkg->vijag', derivative, reshaped_array, precision=highest)
    volume = jnp.einsum('wv,vijkg->wijkg', flux_jac[0], along_x, precision=highest)
    volume = volume + jnp.einsum('wv,vijkg->wijkg', flux_jac[1], along_y, precision=highest)
    volume = volume + jnp.einsum('wv,vijkg->wijkg', flux_jac[2], along_z, precision=highest)
    scale = nodes * (nodes - 1) / 4.0
    repeated = jnp.repeat(match, EX, axis=0).astype(jnp.int32)
    leading = (jnp.arange(layers) % EX == 0)[:, None]
    identity_map = jnp.arange(cells, dtype=jnp.int32)[None, :]
    full_map = jnp.where(leading, repeated, identity_map).astype(jnp.int32)
    inverse_map = jnp.argsort(full_map, axis=-1).astype(jnp.int32)
    low_x = reshaped_array[:, 0]
    high_x = reshaped_array[:, nodes - 1]
    split_low = low_x.reshape(width, nodes, nodes, layers, cells)
    split_high = high_x.reshape(width, nodes, nodes, layers, cells)
    empty_layer = jnp.zeros_like(split_high[:, :, :, :1])
    below = jnp.concatenate([empty_layer, split_high[:, :, :, :-1]], axis=3)
    below = jnp.take_along_axis(below, full_map[None, None, None], axis=4).reshape(width, nodes, nodes, total)
    above = jnp.take_along_axis(split_low, inverse_map[None, None, None], axis=4)
    above = jnp.concatenate([above[:, :, :, 1:], empty_layer], axis=3).reshape(width, nodes, nodes, total)
    low_y = reshaped_array[:, :, 0]
    high_y = reshaped_array[:, :, nodes - 1]
    low_z = reshaped_array[:, :, :, 0]
    high_z = reshaped_array[:, :, :, nodes - 1]

    def across(trace, face_row):
        split = trace.reshape(width, nodes, nodes, layers, cells)
        return jnp.take(split, cross_nbr[face_row], axis=4).reshape(width, nodes, nodes, total)
    volume = volume.at[:, 0].add(scale * surface_term(below, low_x, flux_jac[0], -1.0))
    volume = volume.at[:, nodes - 1].add(scale * surface_term(above, high_x, flux_jac[0], 1.0))
    volume = volume.at[:, :, 0].add(scale * surface_term(across(high_y, 0), low_y, flux_jac[1], -1.0))
    volume = volume.at[:, :, nodes - 1].add(scale * surface_term(across(low_y, 1), high_y, flux_jac[1], 1.0))
    volume = volume.at[:, :, :, 0].add(scale * surface_term(across(high_z, 2), low_z, flux_jac[2], -1.0))
    volume = volume.at[:, :, :, nodes - 1].add(scale * surface_term(across(low_z, 3), high_z, flux_jac[2], 1.0))
    return volume.reshape(field.shape[0], total)

def time_derivative(field):
    count = field.shape[0]
    spectrum = jnp.fft.rfft(field, axis=0)
    waves = jnp.arange(count // 2 + 1)
    factor = jnp.where(waves < count // 2, waves, 0) * frequency
    scaled = spectrum * (1j * factor)[:, None, None]
    return jnp.fft.irfft(scaled, n=count, axis=0).astype(jnp.float32)

def reference(state, forcing, flux_jac, jacobi_inv, cross_nbr, lower_match):
    derivative = jnp.asarray(lobatto_derivative(NODE1), jnp.float32)

    def instance_space(pieces):
        return spatial_residual(pieces[0], flux_jac, derivative, cross_nbr, pieces[1])

    def instance_update(pieces):
        return jnp.dot(pieces[0], pieces[1], preferred_element_type=jnp.float32, precision=lax.Precision.HIGHEST)
    current = state
    first_residual = state
    for sweep in range(SWEEPS):
        residual = lax.map(instance_space, (current, lower_match)) + time_derivative(current) - forcing
        if sweep == 0:
            first_residual = residual
        current = current - lax.map(instance_update, (jacobi_inv, residual))
    return (first_residual, current)
```

```python
import functools
import math

import jax
import jax.numpy as jnp
import numpy as np
from jax import lax
from jax.experimental import pallas as pl
from jax.experimental.pallas import tpu as pltpu
from jax.sharding import PartitionSpec as P

NODE1 = 4
SWEEPS = 2
DISSIPATION = 0.6
FREQUENCY = 0.25
LANES = 128
MESH = pl.DeviceIdType.MESH
BF = jnp.bfloat16
F32 = jnp.float32


def lobatto_derivative(count_of_nodes):
    inner_point = math.sqrt(0.2)
    points = np.array([-1.0, -inner_point, inner_point, 1.0])
    bary = np.ones(count_of_nodes)
    for a in range(count_of_nodes):
        for b in range(count_of_nodes):
            if a != b:
                bary[a] = bary[a] / (points[a] - points[b])
    table = np.zeros((count_of_nodes, count_of_nodes))
    for a in range(count_of_nodes):
        for b in range(count_of_nodes):
            if a != b:
                table[a, b] = bary[b] / bary[a] / (points[a] - points[b])
        table[a, a] = -np.sum(table[a])
    return table


def node_matrices():
    n = NODE1
    scale = n * (n - 1) / 4.0
    der = lobatto_derivative(n).astype(np.float32).astype(np.float64)
    eye = np.eye(n)
    low, high = np.zeros((n, n)), np.zeros((n, n))
    low[0, 0] = 1.0
    high[n - 1, n - 1] = 1.0
    to_low, to_high = np.zeros((n, n)), np.zeros((n, n))
    to_low[0, n - 1] = 1.0
    to_high[n - 1, 0] = 1.0

    def place(m, d):
        parts = [eye, eye, eye]
        parts[d] = m
        return np.kron(np.kron(parts[0], parts[1]), parts[2])

    own = [place(der + scale * (low - high), d) for d in range(3)]
    own.append(DISSIPATION * scale * sum(place(low + high, d) for d in range(3)))
    for d in range(3):
        own.append(place(scale * (to_high - to_low), d))
        own.append(-DISSIPATION * scale * place(to_high + to_low, d))
    return np.stack(own).astype(np.float32)


def time_weights(count):
    half = count // 2
    d = np.zeros(count)
    for m in range(1, count):
        d[m] = 0.5 * FREQUENCY * (-1.0) ** m / math.tan(math.pi * m / count)
    d[half] = 0.0
    plus = np.zeros((half, half))
    minus = np.zeros((half, half))
    for t in range(half):
        for s in range(half):
            a, b = d[(t - s) % count], d[(t - s + half) % count]
            plus[t, s] = 0.5 * (a + b)
            minus[t, s] = 0.5 * (a - b)
    return plus, minus


def split(x):
    hi = x.astype(BF)
    return hi, (x - hi.astype(F32)).astype(BF)


def mm(a, b):
    return jnp.dot(a, b, preferred_element_type=F32)


def kernel(
    cfg, flux_hbm, nodes_hbm, cross_hbm, match_hbm, state_hbm, forcing_hbm, jac_hbm, res, upd,
    xbuf, ybuf, dbuf, halo, match_up, v1, spat1, forc, jac, jcat, vh, vl, wh, wl, py, pz, pb, pa,
    flux, nodes, cross, match, state, send_sem, frecv, brecv, hrecv, mrecv, lsem,
):
    n, ns, T, width, rows, arows, count, cells = cfg
    brows = rows - arows
    block = width * 64
    me = lax.axis_index("inst")
    sp = lax.axis_index("space")
    right, left = lax.rem(sp + 1, ns), lax.rem(sp + ns - 1, ns)
    offsets = sorted(range(1, n), key=lambda k: (-min(k, n - k), k))
    peers = [lax.rem(me + k, n) for k in offsets]

    barrier = pltpu.get_barrier_semaphore()
    for p in peers:
        pl.semaphore_signal(barrier, inc=1, device_id={"inst": p}, device_id_type=MESH)
    for p in (right, left):
        pl.semaphore_signal(barrier, inc=1, device_id={"space": p}, device_id_type=MESH)

    pairs = (
        (state_hbm, state), (match_hbm, match), (cross_hbm, cross), (flux_hbm, flux),
        (nodes_hbm, nodes), (forcing_hbm, forc), (jac_hbm, jac),
    )
    loads = [pltpu.make_async_copy(a, b, lsem.at[i]) for i, (a, b) in enumerate(pairs)]
    for load in loads:
        load.start()
    load_s, load_m, load_c, load_x, load_n, load_f, load_j = loads
    load_s.wait()
    load_m.wait()
    pl.semaphore_wait(barrier, n + 1)

    padded = n * rows != block
    exact0 = state
    if padded:
        for t in range(T):
            v1[0, t, 0:block, :] = state[t]
            v1[0, t, block:, :] = jnp.zeros((n * rows - block, LANES), F32)
            v1[1, t, block:, :] = jnp.zeros((n * rows - block, LANES), F32)
        exact0 = v1.at[0]

    def forward(sweep, src, k, c):
        p = peers[k]
        if c < T:
            t0, nt, r0, nr = c, 1, 0, arows
        else:
            t0, nt, r0, nr = 0, T, arows, brows
        return pltpu.make_async_remote_copy(
            src_ref=src.at[pl.ds(t0, nt), pl.ds(pl.multiple_of(p * rows + r0, 8), nr), :],
            dst_ref=xbuf.at[sweep, pl.ds(me * T + t0, nt), pl.ds(r0, nr), :],
            send_sem=send_sem.at[sweep, 0],
            recv_sem=frecv.at[sweep, c // T],
            device_id={"inst": p},
            device_id_type=MESH,
        )

    def backward(sweep, k, c):
        p = peers[k]
        if c < T:
            t0, nt, r0, nr = c, 1, arows, brows
        else:
            t0, nt, r0, nr = 0, T, 0, arows
        return pltpu.make_async_remote_copy(
            src_ref=ybuf.at[sweep, pl.ds(p * T + t0, nt), pl.ds(r0, nr), :],
            dst_ref=dbuf.at[sweep, pl.ds(t0, nt), pl.ds(pl.multiple_of(me * rows + r0, 8), nr), :],
            send_sem=send_sem.at[sweep, 1],
            recv_sem=brecv.at[sweep, c],
            device_id={"inst": p},
            device_id_type=MESH,
        )

    everyone = range(n - 1)
    others = pl.ds(0, (n - 1) * T)

    def drain(view, sem):
        pltpu.make_async_copy(view, view, sem).wait()

    def wait_forward(sweep, part):
        at = pl.ds(arows, brows) if part else pl.ds(0, arows)
        drain(xbuf.at[sweep, others, at, :], frecv.at[sweep, part])

    def wait_backward(sweep, c):
        if c == T:
            drain(dbuf.at[sweep, :, pl.ds(0, (n - 1) * arows), :], brecv.at[sweep, T])
        else:
            drain(dbuf.at[sweep, c, pl.ds(0, (n - 1) * brows), :], brecv.at[sweep, c])

    def halos(sweep, src):
        out = []
        for t in range(T):
            for v in range(width):
                up = v * 64 + 48
                down = v * 64
                out.append(pltpu.make_async_remote_copy(
                    src_ref=src.at[t, pl.ds(up, 16), :],
                    dst_ref=halo.at[sweep, 0, t, pl.ds(v * 16, 16), :],
                    send_sem=send_sem.at[sweep, 2],
                    recv_sem=hrecv.at[sweep],
                    device_id={"space": right}, device_id_type=MESH))
                out.append(pltpu.make_async_remote_copy(
                    src_ref=src.at[t, pl.ds(down, 16), :],
                    dst_ref=halo.at[sweep, 1, t, pl.ds(v * 16, 16), :],
                    send_sem=send_sem.at[sweep, 2],
                    recv_sem=hrecv.at[sweep],
                    device_id={"space": left}, device_id_type=MESH))
        return out

    send_match = pltpu.make_async_remote_copy(
        src_ref=match, dst_ref=match_up, send_sem=mrecv.at[0], recv_sem=mrecv.at[1],
        device_id={"space": left}, device_id_type=MESH)

    plus, minus = time_weights(count)
    half = count // 2

    def derive(sweep, first, size):
        def group(g, _):
            at = pl.ds(pl.multiple_of(first + g * 8, 8), 8)
            low = [xbuf[sweep, s, at, :] for s in range(half)]
            high = [xbuf[sweep, s + half, at, :] for s in range(half)]
            sums = [a + b for a, b in zip(low, high)]
            diffs = [a - b for a, b in zip(low, high)]
            for t in range(half):
                acc, dif = None, None
                for s in range(half):
                    if abs(plus[t, s]) > 1e-12:
                        term = sums[s] * float(plus[t, s])
                        acc = term if acc is None else acc + term
                    if abs(minus[t, s]) > 1e-12:
                        term = diffs[s] * float(minus[t, s])
                        dif = term if dif is None else dif + term
                ybuf[sweep, t, at, :] = acc + dif
                ybuf[sweep, t + half, at, :] = acc - dif
            return 0
        lax.fori_loop(0, size // 8, group, 0)

    src_row = lax.broadcasted_iota(jnp.int32, (LANES, LANES), 0)
    dst_col = lax.broadcasted_iota(jnp.int32, (LANES, LANES), 1)

    def onehot(mask):
        return jnp.where(mask, 1.0, 0.0).astype(F32)

    def build_weights():
        lane_var = lax.broadcasted_iota(jnp.int32, (1, block), 1) // 64
        tiles = [jnp.concatenate([nodes[i]] * width, axis=1) for i in range(10)]
        for w in range(width):
            fe = []
            for d in range(3):
                row = jnp.zeros((1, block), F32)
                for v in range(width):
                    row = jnp.where(lane_var == v, flux[w, d:d + 1, v:v + 1], row)
                fe.append(row)
            same = jnp.where(lane_var == w, 1.0, 0.0)
            parts = [fe[0] * tiles[0] + fe[1] * tiles[1] + fe[2] * tiles[2] + same * tiles[3]]
            for d in range(3):
                parts.append(fe[d] * tiles[4 + 2 * d] + same * tiles[5 + 2 * d])
            hi, lo = split(jnp.concatenate(parts, axis=1))
            wh[w * 64:(w + 1) * 64, :] = hi
            wl[w * 64:(w + 1) * 64, :] = lo

    def build_moves():
        layer = (lax.broadcasted_iota(jnp.int32, (1, LANES), 1) // cells) * cells
        for f in range(4):
            nb = cross[f:f + 1, :]
            nb = jnp.concatenate([nb] * (LANES // cells), axis=1) + layer
            ref = py if f < 2 else pz
            ref[(f % 2) * LANES:(f % 2 + 1) * LANES, :] = onehot(src_row == nb).astype(BF)

    def build_match():
        last = LANES - cells
        low_ok = jnp.where(sp > 0, 1.0, 0.0)
        high_ok = jnp.where(sp < ns - 1, 1.0, 0.0)
        shift_up = onehot(dst_col == src_row + cells).astype(BF)
        shift_down = onehot(src_row == dst_col + cells).astype(BF)
        for t in range(T):
            m = jnp.concatenate([match[t]] * (LANES // cells), axis=1)
            mu = jnp.concatenate([match_up[t]] * (LANES // cells), axis=1)
            pb[t, 0:LANES, :] = shift_up
            pb[t, LANES:, :] = (onehot((dst_col < cells) & (src_row == m + last)) * low_ok).astype(BF)
            pa[t, 0:LANES, :] = shift_down
            turned = onehot((dst_col < cells) & (src_row == mu + last)) * high_ok
            pa[t, LANES:, :] = turned.T.astype(BF)

    row_id = lax.broadcasted_iota(jnp.int32, (block, 1), 0)

    def as_mask(index, value):
        return jnp.where(index == value, 1.0, 0.0).astype(F32)

    mj3, mj0 = as_mask((row_id >> 2) & 3, 3), as_mask((row_id >> 2) & 3, 0)
    mk3, mk0 = as_mask(row_id & 3, 3), as_mask(row_id & 3, 0)

    def spread_cross(src, t):
        cols = slice(t * LANES, (t + 1) * LANES)
        x = src[t, 0:block, :]
        for part, out in zip(split(x), (vh, vl)):
            out[0:block, cols] = part
            wide = part.astype(F32)
            y = jnp.concatenate([wide * mj3, wide * mj0], axis=1).astype(BF)
            z = jnp.concatenate([wide * mk3, wide * mk0], axis=1).astype(BF)
            out[2 * block:3 * block, cols] = mm(y, py[...]).astype(BF)
            out[3 * block:4 * block, cols] = mm(z, pz[...]).astype(BF)

    def spread_flow(sweep, src, t):
        cols = slice(t * LANES, (t + 1) * LANES)
        own_high = jnp.concatenate([src[t, v * 64 + 48:v * 64 + 64, :] for v in range(width)], axis=0)
        own_low = jnp.concatenate([src[t, v * 64:v * 64 + 16, :] for v in range(width)], axis=0)
        high = split(jnp.concatenate([own_high, halo[sweep, 0, t]], axis=1))
        low = split(jnp.concatenate([own_low, halo[sweep, 1, t]], axis=1))
        for i, out in enumerate((vh, vl)):
            ub = mm(high[i], pb[t]).astype(BF)
            ua = mm(low[i], pa[t]).astype(BF)
            for v in range(width):
                base = block + v * 64
                out[base:base + 16, cols] = ua[v * 16:(v + 1) * 16]
                out[base + 48:base + 64, cols] = ub[v * 16:(v + 1) * 16]

    def clear_middle():
        for out in (vh, vl):
            for v in range(width):
                base = block + v * 64 + 16
                out[base:base + 32, :] = jnp.zeros((32, T * LANES), BF)

    def split_jac():
        load_j.wait()
        for t in range(T):
            hi, lo = split(jac[t])
            jcat[t] = jnp.concatenate([hi, lo, hi], axis=1)

    def apply_space(spat):
        total = mm(wh[...], vh[...]) + mm(wl[...], vh[...]) + mm(wh[...], vl[...])
        for t in range(T):
            spat[t] = total[:, t * LANES:(t + 1) * LANES] - forc[t]

    own_rows = pl.ds(pl.multiple_of(me * rows, 8), rows)
    own_times = pl.ds(me * T, T)

    def run_sweep(sweep, src, before, between):
        xbuf[sweep, own_times, :, :] = src[:, own_rows, :]
        for job in before:
            job()
        wait_forward(sweep, 0)
        derive(sweep, 0, arows)
        for k in everyone:
            backward(sweep, k, T).start()
        for job in between:
            job()
        wait_forward(sweep, 1)
        derive(sweep, arows, brows)
        for c in range(T):
            for k in everyone:
                backward(sweep, k, c).start()
        dbuf[sweep, :, own_rows, :] = ybuf[sweep, own_times, :, :]

    def finish(sweep, src, spat, dst, after):
        wait_backward(sweep, T)
        for t in range(T):
            wait_backward(sweep, t)
            r = spat[t] + dbuf[sweep, t, 0:block, :]
            if sweep == 0:
                spat[t] = r
            hi, lo = split(r)
            step = mm(jcat[t], jnp.concatenate([hi, hi, lo], axis=0))
            dst[t, 0:block, :] = src[t, 0:block, :] - step
            after(t)

    def send_forward(sweep, src, c):
        for k in everyone:
            forward(sweep, src, k, c).start()

    def wait_halos(sweep, src):
        drain(halo.at[sweep], hrecv.at[sweep])

    def first_halo_ready():
        send_match.wait()
        wait_halos(0, state)
        build_match()

    for c in range(T + 1):
        send_forward(0, exact0, c)
    send_match.start()
    for h in halos(0, state):
        h.start()
    before = [load_c.wait, build_moves, load_n.wait, load_x.wait, build_weights]
    before += [functools.partial(spread_cross, state, t) for t in range(T)]
    before += [clear_middle]
    between = [first_halo_ready]
    between += [functools.partial(spread_flow, 0, state, t) for t in range(T)]
    between += [load_f.wait, functools.partial(apply_space, res), split_jac]
    run_sweep(0, exact0, before, between)
    cur = v1.at[1]
    finish(0, state, res, cur, lambda t: send_forward(1, cur, t))

    send_forward(1, cur, T)
    for h in halos(1, cur):
        h.start()
    before = [functools.partial(spread_cross, cur, t) for t in range(T)]
    between = [functools.partial(wait_halos, 1, cur)]
    between += [functools.partial(spread_flow, 1, cur, t) for t in range(T)]
    between += [functools.partial(apply_space, spat1)]
    run_sweep(1, cur, before, between)
    finish(1, cur, spat1, upd, lambda t: None)
    for sweep in range(SWEEPS):
        for i in range(2):
            drain(xbuf.at[sweep, others, :, :], send_sem.at[sweep, i])
        drain(halo.at[sweep], send_sem.at[sweep, 2])


def hand_out(res_vmem, upd_vmem, res_hbm, upd_hbm, sem):
    copies = [
        pltpu.make_async_copy(res_vmem, res_hbm, sem.at[0]),
        pltpu.make_async_copy(upd_vmem, upd_hbm, sem.at[1]),
    ]
    for copy in copies:
        copy.start()
    for copy in copies:
        copy.wait()


def body(n, ns, state, forcing, flux_jac, jacobi_inv, cross_nbr, lower_match):
    T, block, elements = state.shape
    width = flux_jac.shape[1]
    cells = cross_nbr.shape[1]
    count = n * T
    rows = -(-block // (8 * n)) * 8
    arows = -(-rows // 16) * 8
    halo_rows = width * 16
    flux = flux_jac.transpose(1, 0, 2)
    nodes = jnp.asarray(node_matrices())
    cfg = (n, ns, T, width, rows, arows, count, cells)
    full = n * rows
    dma = pltpu.SemaphoreType.DMA
    vmem = pl.BlockSpec(memory_space=pltpu.VMEM)
    hbm = pl.BlockSpec(memory_space=pl.ANY)
    held = pltpu.VMEM(state.shape, F32)
    res, upd = pl.pallas_call(
        functools.partial(kernel, cfg),
        name="sweeps",
        out_shape=(held, held),
        in_specs=[hbm] * 7,
        out_specs=(vmem, vmem),
        scratch_shapes=[
            pltpu.VMEM((SWEEPS, count, rows, LANES), F32),
            pltpu.VMEM((SWEEPS, count, rows, LANES), F32),
            pltpu.VMEM((SWEEPS, T, full, LANES), F32),
            pltpu.VMEM((SWEEPS, 2, T, halo_rows, LANES), F32),
            pltpu.VMEM((T, 1, cells), jnp.int32),
            pltpu.VMEM((2, T, full, LANES), F32),
            pltpu.VMEM((T, block, LANES), F32),
            pltpu.VMEM((T, block, LANES), F32),
            pltpu.VMEM((T, block, block), F32),
            pltpu.VMEM((T, block, 3 * block), BF),
            pltpu.VMEM((4 * block, T * LANES), BF),
            pltpu.VMEM((4 * block, T * LANES), BF),
            pltpu.VMEM((block, 4 * block), BF),
            pltpu.VMEM((block, 4 * block), BF),
            pltpu.VMEM((2 * LANES, LANES), BF),
            pltpu.VMEM((2 * LANES, LANES), BF),
            pltpu.VMEM((T, 2 * LANES, LANES), BF),
            pltpu.VMEM((T, 2 * LANES, LANES), BF),
            pltpu.VMEM(flux.shape, F32),
            pltpu.VMEM(nodes.shape, F32),
            pltpu.VMEM(cross_nbr.shape, jnp.int32),
            pltpu.VMEM(lower_match.shape, jnp.int32),
            pltpu.VMEM((T, block, LANES), F32),
            dma((SWEEPS, 3)),
            dma((SWEEPS, 2)),
            dma((SWEEPS, T + 1)),
            dma((SWEEPS,)),
            dma((2,)),
            dma((7,)),
        ],
        compiler_params=pltpu.CompilerParams(
            collective_id=0, has_side_effects=True, vmem_limit_bytes=56 * 1024 * 1024
        ),
    )(flux, nodes, cross_nbr, lower_match, state, forcing, jacobi_inv)
    out = jax.ShapeDtypeStruct(state.shape, F32)
    return pl.pallas_call(
        hand_out,
        name="hand_out",
        out_shape=(out, out),
        in_specs=[vmem] * 2,
        out_specs=(hbm, hbm),
        scratch_shapes=[dma((2,))],
    )(pltpu.with_memory_space_constraint(res, pltpu.VMEM), pltpu.with_memory_space_constraint(upd, pltpu.VMEM))


def solution(mesh):
    n, ns = mesh.shape["inst"], mesh.shape["space"]
    return jax.shard_map(
        functools.partial(body, n, ns),
        mesh=mesh,
        in_specs=(
            P("inst", None, "space"),
            P("inst", None, "space"),
            P(),
            P("inst", None, None),
            P(),
            P("inst", "space", None),
        ),
        out_specs=(P("inst", None, "space"), P("inst", None, "space")),
        check_vma=False,
    )
```

```python
import functools
import math

import jax
import jax.numpy as jnp
import numpy as np
from jax import lax
from jax.experimental import pallas as pl
from jax.experimental.pallas import tpu as pltpu
from jax.sharding import PartitionSpec as P

NODE1 = 4
SWEEPS = 2
DISSIPATION = 0.6
FREQUENCY = 0.25
LANES = 128
MESH = pl.DeviceIdType.MESH
BF = jnp.bfloat16
F32 = jnp.float32


def lobatto_derivative(count_of_nodes):
    inner_point = math.sqrt(0.2)
    points = np.array([-1.0, -inner_point, inner_point, 1.0])
    bary = np.ones(count_of_nodes)
    for a in range(count_of_nodes):
        for b in range(count_of_nodes):
            if a != b:
                bary[a] = bary[a] / (points[a] - points[b])
    table = np.zeros((count_of_nodes, count_of_nodes))
    for a in range(count_of_nodes):
        for b in range(count_of_nodes):
            if a != b:
                table[a, b] = bary[b] / bary[a] / (points[a] - points[b])
        table[a, a] = -np.sum(table[a])
    return table


def node_matrices():
    n = NODE1
    scale = n * (n - 1) / 4.0
    der = lobatto_derivative(n).astype(np.float32).astype(np.float64)
    eye = np.eye(n)
    low, high = np.zeros((n, n)), np.zeros((n, n))
    low[0, 0] = 1.0
    high[n - 1, n - 1] = 1.0
    to_low, to_high = np.zeros((n, n)), np.zeros((n, n))
    to_low[0, n - 1] = 1.0
    to_high[n - 1, 0] = 1.0

    def place(m, d):
        parts = [eye, eye, eye]
        parts[d] = m
        return np.kron(np.kron(parts[0], parts[1]), parts[2])

    own = [place(der + scale * (low - high), d) for d in range(3)]
    own.append(DISSIPATION * scale * sum(place(low + high, d) for d in range(3)))
    for d in range(3):
        own.append(place(scale * (to_high - to_low), d))
        own.append(-DISSIPATION * scale * place(to_high + to_low, d))
    return np.stack(own).astype(np.float32)


def time_weights(count):
    half = count // 2
    d = np.zeros(count)
    for m in range(1, count):
        d[m] = 0.5 * FREQUENCY * (-1.0) ** m / math.tan(math.pi * m / count)
    d[half] = 0.0
    plus = np.zeros((half, half))
    minus = np.zeros((half, half))
    for t in range(half):
        for s in range(half):
            a, b = d[(t - s) % count], d[(t - s + half) % count]
            plus[t, s] = 0.5 * (a + b)
            minus[t, s] = 0.5 * (a - b)
    return plus, minus


def split(x):
    hi = x.astype(BF)
    return hi, (x - hi.astype(F32)).astype(BF)


def mm(a, b):
    return jnp.dot(a, b, preferred_element_type=F32)


def kernel(
    cfg, flux_hbm, nodes_hbm, cross_hbm, match_hbm, state_hbm, forcing_hbm, jac_hbm, res, upd,
    xbuf, ybuf, dbuf, halo, match_up, v1, spat1, part, forc, jac, jone, jtwo, vh, vl, wh, wl, py, pz, pb, pa,
    flux, nodes, cross, match, state, send_sem, frecv, brecv, hrecv, mrecv, lsem,
):
    n, ns, T, width, rows, arows, count, cells = cfg
    brows = rows - arows
    block = width * 64
    first = [(p * rows, min(arows, block - p * rows)) for p in range(n) if p * rows < block]
    second = [(p * rows + arows, min(brows, block - p * rows - arows)) for p in range(n) if p * rows + arows < block]
    early = sum(size for _, size in first)
    me = lax.axis_index("inst")
    sp = lax.axis_index("space")
    right, left = lax.rem(sp + 1, ns), lax.rem(sp + ns - 1, ns)
    side, quarter = n // 2, n // 4
    high = jnp.where(me >= side, 1, 0)
    own, other = high * side, (1 - high) * side
    inner, odd = me - own, me % 2
    peers = [other + lax.rem(k + odd * (1 - 2 * (k % 2)) + (1 - high) * quarter, side) for k in range(side)]
    peers += [own + lax.rem(inner + k, side) for k in (*range(quarter, side), *range(1, quarter))]
    edge = (me < quarter) | (me >= n - quarter)

    barrier = pltpu.get_barrier_semaphore()
    for p in peers:
        pl.semaphore_signal(barrier, inc=1, device_id={"inst": p}, device_id_type=MESH)
    for p in (right, left):
        pl.semaphore_signal(barrier, inc=1, device_id={"space": p}, device_id_type=MESH)

    pairs = (
        (state_hbm, state), (match_hbm, match), (cross_hbm, cross), (flux_hbm, flux),
        (nodes_hbm, nodes), (forcing_hbm, forc), (jac_hbm, jac),
    )
    loads = [pltpu.make_async_copy(a, b, lsem.at[i]) for i, (a, b) in enumerate(pairs)]
    load_s, load_m, load_c, load_x, load_n, load_f, load_j = loads
    load_s.start()
    load_m.start()
    load_s.wait()
    load_m.wait()
    pl.semaphore_wait(barrier, n + 1)

    padded = n * rows != block
    exact0 = state
    if padded:
        for t in range(T):
            v1[0, t, 0:block, :] = state[t]
            v1[0, t, block:, :] = jnp.zeros((n * rows - block, LANES), F32)
            v1[1, t, block:, :] = jnp.zeros((n * rows - block, LANES), F32)
        exact0 = v1.at[0]

    def forward(sweep, src, k, c):
        p = peers[k]
        if sweep == 0 and c == 0:
            t0, nt, r0, nr = 0, T, 0, arows
        elif c < T:
            t0, nt, r0, nr = c, 1, 0, arows
        else:
            t0, nt, r0, nr = 0, T, arows, brows
        return pltpu.make_async_remote_copy(
            src_ref=src.at[pl.ds(t0, nt), pl.ds(pl.multiple_of(p * rows + r0, 8), nr), :],
            dst_ref=xbuf.at[sweep, pl.ds(me * T + t0, nt), pl.ds(r0, nr), :],
            send_sem=send_sem.at[sweep, 0],
            recv_sem=frecv.at[sweep, c // T],
            device_id={"inst": p},
            device_id_type=MESH,
        )

    def piece(sweep, k, part, t0, nt, sem):
        p = peers[k]
        r0, nr = ((0, arows), (arows, brows))[part]
        return pltpu.make_async_remote_copy(
            src_ref=ybuf.at[sweep, pl.ds(p * T + t0, nt), pl.ds(r0, nr), :],
            dst_ref=dbuf.at[sweep, pl.ds(t0, nt), pl.ds(pl.multiple_of(me * rows + r0, 8), nr), :],
            send_sem=send_sem.at[sweep, 1],
            recv_sem=brecv.at[sweep, sem],
            device_id={"inst": p},
            device_id_type=MESH,
        )

    def backward(k, c):
        if c < T:
            return piece(0, k, 1, c, 1, c)
        return piece(0, k, 0, 0, T, T)

    def backward_last(k, part, g):
        t0, nt = groups[g]
        return piece(SWEEPS - 1, k, part, t0, nt, 2 * g + part)

    everyone = range(n - 1)
    groups = [(t0, min(2, T - t0)) for t0 in range(0, T, 2)]
    others = pl.ds(0, (n - 1) * T)

    def drain(view, sem):
        pltpu.make_async_copy(view, view, sem).wait()

    def wait_forward(sweep, part):
        at = pl.ds(arows, brows) if part else pl.ds(0, arows)
        drain(xbuf.at[sweep, others, at, :], frecv.at[sweep, part])

    def wait_backward(c):
        if c == T:
            drain(dbuf.at[0, :, pl.ds(0, (n - 1) * arows), :], brecv.at[0, T])
        else:
            drain(dbuf.at[0, c, pl.ds(0, (n - 1) * brows), :], brecv.at[0, c])

    def wait_last(g, part):
        t0, nt = groups[g]
        size = (n - 1) * (arows, brows)[part]
        drain(dbuf.at[SWEEPS - 1, pl.ds(t0, nt), pl.ds(0, size), :], brecv.at[SWEEPS - 1, 2 * g + part])

    def halos(sweep, src):
        out = []
        for t in range(T):
            for v in range(width):
                up = v * 64 + 48
                down = v * 64
                out.append(pltpu.make_async_remote_copy(
                    src_ref=src.at[t, pl.ds(up, 16), :],
                    dst_ref=halo.at[sweep, 0, t, pl.ds(v * 16, 16), :],
                    send_sem=send_sem.at[sweep, 2],
                    recv_sem=hrecv.at[sweep],
                    device_id={"space": right}, device_id_type=MESH))
                out.append(pltpu.make_async_remote_copy(
                    src_ref=src.at[t, pl.ds(down, 16), :],
                    dst_ref=halo.at[sweep, 1, t, pl.ds(v * 16, 16), :],
                    send_sem=send_sem.at[sweep, 2],
                    recv_sem=hrecv.at[sweep],
                    device_id={"space": left}, device_id_type=MESH))
        return out

    send_match = pltpu.make_async_remote_copy(
        src_ref=match, dst_ref=match_up, send_sem=mrecv.at[0], recv_sem=mrecv.at[1],
        device_id={"space": left}, device_id_type=MESH)

    plus, minus = time_weights(count)
    half = count // 2

    def derive(sweep, first, size):
        def group(g, _):
            at = pl.ds(pl.multiple_of(first + g * 8, 8), 8)
            low = [xbuf[sweep, s, at, :] for s in range(half)]
            high = [xbuf[sweep, s + half, at, :] for s in range(half)]
            sums = [a + b for a, b in zip(low, high)]
            diffs = [a - b for a, b in zip(low, high)]
            for t in range(half):
                acc, dif = None, None
                for s in range(half):
                    if abs(plus[t, s]) > 1e-12:
                        term = sums[s] * float(plus[t, s])
                        acc = term if acc is None else acc + term
                    if abs(minus[t, s]) > 1e-12:
                        term = diffs[s] * float(minus[t, s])
                        dif = term if dif is None else dif + term
                ybuf[sweep, t, at, :] = acc + dif
                ybuf[sweep, t + half, at, :] = acc - dif
            return 0
        lax.fori_loop(0, size // 8, group, 0)

    src_row = lax.broadcasted_iota(jnp.int32, (LANES, LANES), 0)
    dst_col = lax.broadcasted_iota(jnp.int32, (LANES, LANES), 1)

    def onehot(mask):
        return jnp.where(mask, 1.0, 0.0).astype(F32)

    def build_weights():
        lane_var = lax.broadcasted_iota(jnp.int32, (1, block), 1) // 64
        tiles = [jnp.concatenate([nodes[i]] * width, axis=1) for i in range(10)]
        for w in range(width):
            fe = []
            for d in range(3):
                row = jnp.zeros((1, block), F32)
                for v in range(width):
                    row = jnp.where(lane_var == v, flux[w, d:d + 1, v:v + 1], row)
                fe.append(row)
            same = jnp.where(lane_var == w, 1.0, 0.0)
            parts = [fe[0] * tiles[0] + fe[1] * tiles[1] + fe[2] * tiles[2] + same * tiles[3]]
            for d in range(3):
                parts.append(fe[d] * tiles[4 + 2 * d] + same * tiles[5 + 2 * d])
            hi, lo = split(jnp.concatenate(parts, axis=1))
            wh[w * 64:(w + 1) * 64, :] = hi
            wl[w * 64:(w + 1) * 64, :] = lo

    def build_moves():
        layer = (lax.broadcasted_iota(jnp.int32, (1, LANES), 1) // cells) * cells
        for f in range(4):
            nb = cross[f:f + 1, :]
            nb = jnp.concatenate([nb] * (LANES // cells), axis=1) + layer
            ref = py if f < 2 else pz
            ref[(f % 2) * LANES:(f % 2 + 1) * LANES, :] = onehot(src_row == nb).astype(BF)

    def build_match():
        last = LANES - cells
        low_ok = jnp.where(sp > 0, 1.0, 0.0)
        high_ok = jnp.where(sp < ns - 1, 1.0, 0.0)
        shift_up = onehot(dst_col == src_row + cells).astype(BF)
        shift_down = onehot(src_row == dst_col + cells).astype(BF)
        for t in range(T):
            m = jnp.concatenate([match[t]] * (LANES // cells), axis=1)
            mu = jnp.concatenate([match_up[t]] * (LANES // cells), axis=1)
            pb[t, 0:LANES, :] = shift_up
            pb[t, LANES:, :] = (onehot((dst_col < cells) & (src_row == m + last)) * low_ok).astype(BF)
            pa[t, 0:LANES, :] = shift_down
            turned = onehot((dst_col < cells) & (src_row == mu + last)) * high_ok
            pa[t, LANES:, :] = turned.T.astype(BF)

    row_id = lax.broadcasted_iota(jnp.int32, (block, 1), 0)

    def as_mask(index, value):
        return jnp.where(index == value, 1.0, 0.0).astype(F32)

    mj3, mj0 = as_mask((row_id >> 2) & 3, 3), as_mask((row_id >> 2) & 3, 0)
    mk3, mk0 = as_mask(row_id & 3, 3), as_mask(row_id & 3, 0)

    def spread_cross(src, t):
        cols = slice(t * LANES, (t + 1) * LANES)
        x = src[t, 0:block, :]
        for part, out in zip(split(x), (vh, vl)):
            out[0:block, cols] = part
            wide = part.astype(F32)
            y = jnp.concatenate([wide * mj3, wide * mj0], axis=1).astype(BF)
            z = jnp.concatenate([wide * mk3, wide * mk0], axis=1).astype(BF)
            out[2 * block:3 * block, cols] = mm(y, py[...]).astype(BF)
            out[3 * block:4 * block, cols] = mm(z, pz[...]).astype(BF)

    def spread_flow(sweep, src, t):
        cols = slice(t * LANES, (t + 1) * LANES)
        own_high = jnp.concatenate([src[t, v * 64 + 48:v * 64 + 64, :] for v in range(width)], axis=0)
        own_low = jnp.concatenate([src[t, v * 64:v * 64 + 16, :] for v in range(width)], axis=0)
        high = split(jnp.concatenate([own_high, halo[sweep, 0, t]], axis=1))
        low = split(jnp.concatenate([own_low, halo[sweep, 1, t]], axis=1))
        for i, out in enumerate((vh, vl)):
            ub = mm(high[i], pb[t]).astype(BF)
            ua = mm(low[i], pa[t]).astype(BF)
            for v in range(width):
                base = block + v * 64
                out[base:base + 16, cols] = ua[v * 16:(v + 1) * 16]
                out[base + 48:base + 64, cols] = ub[v * 16:(v + 1) * 16]

    def clear_middle():
        for out in (vh, vl):
            for v in range(width):
                base = block + v * 64 + 16
                out[base:base + 32, :] = jnp.zeros((32, T * LANES), BF)

    def split_jac():
        load_j.wait()
        place = lax.broadcasted_iota(jnp.int32, (block, block), 0)
        column = lax.broadcasted_iota(jnp.int32, (block, block), 1)
        chosen, at = column < 0, 0
        for start, size in first + second:
            chosen = chosen | ((column >= at) & (column < at + size) & (place - column == start - at))
            at += size
        chosen = onehot(chosen).astype(BF)
        for t in range(T):
            hi, lo = [mm(part, chosen).astype(BF) for part in split(jac[t])]
            jone[t] = jnp.concatenate([hi[:, :early], lo[:, :early], hi[:, :early]], axis=1)
            jtwo[t] = jnp.concatenate([hi[:, early:], lo[:, early:], hi[:, early:]], axis=1)

    def apply_space(spat):
        total = mm(wh[...], vh[...]) + mm(wl[...], vh[...]) + mm(wh[...], vl[...])
        for t in range(T):
            spat[t] = total[:, t * LANES:(t + 1) * LANES] - forc[t]

    lead, held, near = range(quarter), range(quarter, side), range(side, n - 1)

    def start_early(sweep):
        if sweep == 0:
            for k in everyone:
                backward(k, T).start()
            return
        for g in range(len(groups)):
            for k in (*lead, *near):
                backward_last(k, 0, g).start()

    def start_late(sweep):
        if sweep == 0:
            for c in range(T):
                for k in everyone:
                    backward(k, c).start()
            return
        for g in range(len(groups)):
            for k in lead:
                backward_last(k, 1, g).start()
        for g in range(len(groups)):
            for k in near:
                backward_last(k, 1, g).start()
        for g in range(len(groups)):
            for part in range(2):
                for k in held:
                    backward_last(k, part, g).start()

    own_rows = pl.ds(pl.multiple_of(me * rows, 8), rows)
    own_times = pl.ds(me * T, T)

    def run_sweep(sweep, src, before, between):
        xbuf[sweep, own_times, :, :] = src[:, own_rows, :]
        for job in before:
            job()
        wait_forward(sweep, 0)
        derive(sweep, 0, arows)
        start_early(sweep)
        for job in between:
            job()
        wait_forward(sweep, 1)
        derive(sweep, arows, brows)
        start_late(sweep)
        dbuf[sweep, :, own_rows, :] = ybuf[sweep, own_times, :, :]

    def step(sweep, spat, t, spans, weights):
        r = []
        for start, size in spans:
            at = slice(start, start + size)
            r.append(spat[t, at, :] + dbuf[sweep, t, at, :])
            if sweep == 0:
                spat[t, at, :] = r[-1]
        hi, lo = split(jnp.concatenate(r, axis=0))
        return mm(weights[t], jnp.concatenate([hi, hi, lo], axis=0))

    def finish(src, spat, dst, after):
        wait_backward(T)
        for t in range(T):
            part[t] = src[t, 0:block, :] - step(0, spat, t, first, jone)
        for t in range(T):
            wait_backward(t)
            dst[t, 0:block, :] = part[t] - step(0, spat, t, second, jtwo)
            after(t)

    def finish_last(src, spat, dst):
        for g, (t0, nt) in enumerate(groups):
            wait_last(g, 0)
            for t in range(t0, t0 + nt):
                part[t] = src[t, 0:block, :] - step(1, spat, t, first, jone)
            wait_last(g, 1)
            for t in range(t0, t0 + nt):
                dst[t, 0:block, :] = part[t] - step(1, spat, t, second, jtwo)

    def send_forward(sweep, src, c):
        for k in everyone:
            forward(sweep, src, k, c).start()

    def wait_halos(sweep, src):
        drain(halo.at[sweep], hrecv.at[sweep])

    def first_halo_ready():
        send_match.wait()
        wait_halos(0, state)
        build_match()

    for c in (0, T):
        send_forward(0, exact0, c)
    for load in loads[2:]:
        load.start()
    send_match.start()
    for h in halos(0, state):
        h.start()
    before = [load_c.wait, build_moves, load_n.wait, load_x.wait, build_weights]
    before += [functools.partial(spread_cross, state, t) for t in range(T)]
    before += [clear_middle]
    between = [first_halo_ready]
    between += [functools.partial(spread_flow, 0, state, t) for t in range(T)]
    between += [load_f.wait, functools.partial(apply_space, res), split_jac]
    run_sweep(0, exact0, before, between)
    cur = v1.at[1]
    finish(state, res, cur, lambda t: send_forward(1, cur, t))

    send_forward(1, cur, T)
    for h in halos(1, cur):
        h.start()
    before = [functools.partial(spread_cross, cur, t) for t in range(T)]
    between = [functools.partial(wait_halos, 1, cur)]
    between += [functools.partial(spread_flow, 1, cur, t) for t in range(T)]
    between += [functools.partial(apply_space, spat1)]
    run_sweep(1, cur, before, between)
    finish_last(cur, spat1, upd)
    for sweep in range(SWEEPS):
        for i in range(2):
            drain(xbuf.at[sweep, others, :, :], send_sem.at[sweep, i])
        drain(halo.at[sweep], send_sem.at[sweep, 2])


def hand_out(res_vmem, upd_vmem, res_hbm, upd_hbm, sem):
    copies = [
        pltpu.make_async_copy(res_vmem, res_hbm, sem.at[0]),
        pltpu.make_async_copy(upd_vmem, upd_hbm, sem.at[1]),
    ]
    for copy in copies:
        copy.start()
    for copy in copies:
        copy.wait()


def body(n, ns, state, forcing, flux_jac, jacobi_inv, cross_nbr, lower_match):
    T, block, elements = state.shape
    width = flux_jac.shape[1]
    cells = cross_nbr.shape[1]
    count = n * T
    rows = -(-block // (8 * n)) * 8
    arows = -(-rows // 16) * 8
    halo_rows = width * 16
    early = sum(max(0, min(arows, block - p * rows)) for p in range(n))
    flux = flux_jac.transpose(1, 0, 2)
    nodes = jnp.asarray(node_matrices())
    cfg = (n, ns, T, width, rows, arows, count, cells)
    full = n * rows
    dma = pltpu.SemaphoreType.DMA
    vmem = pl.BlockSpec(memory_space=pltpu.VMEM)
    hbm = pl.BlockSpec(memory_space=pl.ANY)
    held = pltpu.VMEM(state.shape, F32)
    res, upd = pl.pallas_call(
        functools.partial(kernel, cfg),
        name="sweeps",
        out_shape=(held, held),
        in_specs=[hbm] * 7,
        out_specs=(vmem, vmem),
        scratch_shapes=[
            pltpu.VMEM((SWEEPS, count, rows, LANES), F32),
            pltpu.VMEM((SWEEPS, count, rows, LANES), F32),
            pltpu.VMEM((SWEEPS, T, full, LANES), F32),
            pltpu.VMEM((SWEEPS, 2, T, halo_rows, LANES), F32),
            pltpu.VMEM((T, 1, cells), jnp.int32),
            pltpu.VMEM((2, T, full, LANES), F32),
            pltpu.VMEM((T, block, LANES), F32),
            pltpu.VMEM((T, block, LANES), F32),
            pltpu.VMEM((T, block, LANES), F32),
            pltpu.VMEM((T, block, block), F32),
            pltpu.VMEM((T, block, 3 * early), BF),
            pltpu.VMEM((T, block, 3 * (block - early)), BF),
            pltpu.VMEM((4 * block, T * LANES), BF),
            pltpu.VMEM((4 * block, T * LANES), BF),
            pltpu.VMEM((block, 4 * block), BF),
            pltpu.VMEM((block, 4 * block), BF),
            pltpu.VMEM((2 * LANES, LANES), BF),
            pltpu.VMEM((2 * LANES, LANES), BF),
            pltpu.VMEM((T, 2 * LANES, LANES), BF),
            pltpu.VMEM((T, 2 * LANES, LANES), BF),
            pltpu.VMEM(flux.shape, F32),
            pltpu.VMEM(nodes.shape, F32),
            pltpu.VMEM(cross_nbr.shape, jnp.int32),
            pltpu.VMEM(lower_match.shape, jnp.int32),
            pltpu.VMEM((T, block, LANES), F32),
            dma((SWEEPS, 3)),
            dma((SWEEPS, 2)),
            dma((SWEEPS, T + 1)),
            dma((SWEEPS,)),
            dma((2,)),
            dma((7,)),
        ],
        compiler_params=pltpu.CompilerParams(
            collective_id=0, has_side_effects=True, vmem_limit_bytes=56 * 1024 * 1024
        ),
    )(flux, nodes, cross_nbr, lower_match, state, forcing, jacobi_inv)
    out = jax.ShapeDtypeStruct(state.shape, F32)
    return pl.pallas_call(
        hand_out,
        name="hand_out",
        out_shape=(out, out),
        in_specs=[vmem] * 2,
        out_specs=(hbm, hbm),
        scratch_shapes=[dma((2,))],
    )(pltpu.with_memory_space_constraint(res, pltpu.VMEM), pltpu.with_memory_space_constraint(upd, pltpu.VMEM))


def solution(mesh):
    n, ns = mesh.shape["inst"], mesh.shape["space"]
    return jax.shard_map(
        functools.partial(body, n, ns),
        mesh=mesh,
        in_specs=(
            P("inst", None, "space"),
            P("inst", None, "space"),
            P(),
            P("inst", None, None),
            P(),
            P("inst", "space", None),
        ),
        out_specs=(P("inst", None, "space"), P("inst", None, "space")),
        check_vma=False,
    )
```

```python
import functools
import math

import jax
import jax.numpy as jnp
import numpy as np
from jax import lax
from jax.experimental import pallas as pl
from jax.experimental.pallas import tpu as pltpu
from jax.sharding import PartitionSpec as P

NODE1 = 4
SWEEPS = 2
DISSIPATION = 0.6
FREQUENCY = 0.25
LANES = 128
MESH = pl.DeviceIdType.MESH
BF = jnp.bfloat16
F32 = jnp.float32


def lobatto_derivative(count_of_nodes):
    inner_point = math.sqrt(0.2)
    points = np.array([-1.0, -inner_point, inner_point, 1.0])
    bary = np.ones(count_of_nodes)
    for a in range(count_of_nodes):
        for b in range(count_of_nodes):
            if a != b:
                bary[a] = bary[a] / (points[a] - points[b])
    table = np.zeros((count_of_nodes, count_of_nodes))
    for a in range(count_of_nodes):
        for b in range(count_of_nodes):
            if a != b:
                table[a, b] = bary[b] / bary[a] / (points[a] - points[b])
        table[a, a] = -np.sum(table[a])
    return table


def node_matrices():
    n = NODE1
    scale = n * (n - 1) / 4.0
    der = lobatto_derivative(n).astype(np.float32).astype(np.float64)
    eye = np.eye(n)
    low, high = np.zeros((n, n)), np.zeros((n, n))
    low[0, 0] = 1.0
    high[n - 1, n - 1] = 1.0
    to_low, to_high = np.zeros((n, n)), np.zeros((n, n))
    to_low[0, n - 1] = 1.0
    to_high[n - 1, 0] = 1.0

    def place(m, d):
        parts = [eye, eye, eye]
        parts[d] = m
        return np.kron(np.kron(parts[0], parts[1]), parts[2])

    own = [place(der + scale * (low - high), d) for d in range(3)]
    own.append(DISSIPATION * scale * sum(place(low + high, d) for d in range(3)))
    for d in range(3):
        own.append(place(scale * (to_high - to_low), d))
        own.append(-DISSIPATION * scale * place(to_high + to_low, d))
    return np.stack(own).astype(np.float32)


def time_weights(count):
    half = count // 2
    d = np.zeros(count)
    for m in range(1, count):
        d[m] = 0.5 * FREQUENCY * (-1.0) ** m / math.tan(math.pi * m / count)
    d[half] = 0.0
    plus = np.zeros((half, half))
    minus = np.zeros((half, half))
    for t in range(half):
        for s in range(half):
            a, b = d[(t - s) % count], d[(t - s + half) % count]
            plus[t, s] = 0.5 * (a + b)
            minus[t, s] = 0.5 * (a - b)
    return plus, minus


def split(x):
    hi = x.astype(BF)
    return hi, (x - hi.astype(F32)).astype(BF)


def mm(a, b):
    return jnp.dot(a, b, preferred_element_type=F32)


def kernel(
    cfg, flux_hbm, nodes_hbm, cross_hbm, match_hbm, state_hbm, forcing_hbm, jac_hbm, res, upd,
    xbuf, ybuf, dbuf, halo, match_up, v1, spat1, part, forc, jac, jone, jtwo, vh, vl, wh, wl, py, pz, pb, pa,
    flux, nodes, cross, match, state, send_sem, frecv, brecv, hrecv, mrecv, lsem,
):
    n, ns, T, width, rows, arows, count, cells = cfg
    brows = rows - arows
    block = width * 64
    first = [(p * rows, min(arows, block - p * rows)) for p in range(n) if p * rows < block]
    second = [(p * rows + arows, min(brows, block - p * rows - arows)) for p in range(n) if p * rows + arows < block]
    early = sum(size for _, size in first)
    me = lax.axis_index("inst")
    sp = lax.axis_index("space")
    right, left = lax.rem(sp + 1, ns), lax.rem(sp + ns - 1, ns)
    side, quarter = n // 2, n // 4
    high = jnp.where(me >= side, 1, 0)
    own, other = high * side, (1 - high) * side
    inner, odd = me - own, me % 2
    ranked = [other + lax.rem(k + (1 - high) * quarter, side) for k in range(side)]
    peers = [other + lax.rem(k + odd * (1 - 2 * (k % 2)) + (1 - high) * quarter, side) for k in range(side)]
    peers += [own + lax.rem(inner + k, side) for k in (*range(quarter, side), *range(1, quarter))]

    barrier = pltpu.get_barrier_semaphore()
    for p in peers:
        pl.semaphore_signal(barrier, inc=1, device_id={"inst": p}, device_id_type=MESH)
    for p in (right, left):
        pl.semaphore_signal(barrier, inc=1, device_id={"space": p}, device_id_type=MESH)

    pairs = (
        (state_hbm, state), (match_hbm, match), (cross_hbm, cross), (flux_hbm, flux),
        (nodes_hbm, nodes), (forcing_hbm, forc), (jac_hbm, jac),
    )
    loads = [pltpu.make_async_copy(a, b, lsem.at[i % 5]) for i, (a, b) in enumerate(pairs)]
    load_s, load_m, load_c, load_x, load_n, load_f, load_j = loads
    load_s.start()
    load_m.start()
    load_s.wait()
    load_m.wait()
    pl.semaphore_wait(barrier, n + 1)

    padded = n * rows != block
    exact0 = state
    if padded:
        for t in range(T):
            v1[0, t, 0:block, :] = state[t]
            v1[0, t, block:, :] = jnp.zeros((n * rows - block, LANES), F32)
            v1[1, t, block:, :] = jnp.zeros((n * rows - block, LANES), F32)
        exact0 = v1.at[0]

    def forward(sweep, src, k, c):
        p = peers[k]
        if sweep == 0 and c == 0:
            t0, nt, r0, nr = 0, T, 0, arows
        elif c < T:
            t0, nt, r0, nr = c, 1, 0, arows
        else:
            t0, nt, r0, nr = 0, T, arows, brows
        return pltpu.make_async_remote_copy(
            src_ref=src.at[pl.ds(t0, nt), pl.ds(pl.multiple_of(p * rows + r0, 8), nr), :],
            dst_ref=xbuf.at[sweep, pl.ds(me * T + t0, nt), pl.ds(r0, nr), :],
            send_sem=send_sem.at[0],
            recv_sem=frecv.at[c // T],
            device_id={"inst": p},
            device_id_type=MESH,
        )

    def piece(sweep, k, part, t0, nt, sem):
        p = ranked[k] if sweep > 0 and k < side else peers[k]
        r0, nr = ((0, arows), (arows, brows))[part]
        return pltpu.make_async_remote_copy(
            src_ref=ybuf.at[sweep, pl.ds(p * T + t0, nt), pl.ds(r0, nr), :],
            dst_ref=dbuf.at[sweep, pl.ds(t0, nt), pl.ds(pl.multiple_of(me * rows + r0, 8), nr), :],
            send_sem=send_sem.at[1],
            recv_sem=brecv.at[sem],
            device_id={"inst": p},
            device_id_type=MESH,
        )

    def backward(k, c):
        if c < T:
            return piece(0, k, 1, c, 1, c)
        return piece(0, k, 0, 0, T, T)

    def backward_last(k, part, g):
        t0, nt = groups[g]
        return piece(SWEEPS - 1, k, part, t0, nt, 2 * g + part)

    everyone = range(n - 1)
    groups = [(t0, min(2, T - t0)) for t0 in range(0, T, 2)]
    others = pl.ds(0, (n - 1) * T)

    def drain(view, sem):
        pltpu.make_async_copy(view, view, sem).wait()

    def wait_forward(sweep, part):
        at = pl.ds(arows, brows) if part else pl.ds(0, arows)
        drain(xbuf.at[sweep, others, at, :], frecv.at[part])

    def wait_backward(c):
        if c == T:
            drain(dbuf.at[0, :, pl.ds(0, (n - 1) * arows), :], brecv.at[T])
        else:
            drain(dbuf.at[0, c, pl.ds(0, (n - 1) * brows), :], brecv.at[c])

    def wait_last(g, part):
        t0, nt = groups[g]
        size = (n - 1) * (arows, brows)[part]
        drain(dbuf.at[SWEEPS - 1, pl.ds(t0, nt), pl.ds(0, size), :], brecv.at[2 * g + part])

    def halos(sweep, src):
        out = []
        for t in range(T):
            for v in range(width):
                up = v * 64 + 48
                down = v * 64
                out.append(pltpu.make_async_remote_copy(
                    src_ref=src.at[t, pl.ds(up, 16), :],
                    dst_ref=halo.at[sweep, 0, t, pl.ds(v * 16, 16), :],
                    send_sem=send_sem.at[2],
                    recv_sem=hrecv.at[sweep],
                    device_id={"space": right}, device_id_type=MESH))
                out.append(pltpu.make_async_remote_copy(
                    src_ref=src.at[t, pl.ds(down, 16), :],
                    dst_ref=halo.at[sweep, 1, t, pl.ds(v * 16, 16), :],
                    send_sem=send_sem.at[2],
                    recv_sem=hrecv.at[sweep],
                    device_id={"space": left}, device_id_type=MESH))
        return out

    send_match = pltpu.make_async_remote_copy(
        src_ref=match, dst_ref=match_up, send_sem=mrecv.at[0], recv_sem=mrecv.at[1],
        device_id={"space": left}, device_id_type=MESH)

    plus, minus = time_weights(count)
    half = count // 2

    def derive(sweep, first, size):
        def group(g, _):
            at = pl.ds(pl.multiple_of(first + g * 8, 8), 8)
            low = [xbuf[sweep, s, at, :] for s in range(half)]
            high = [xbuf[sweep, s + half, at, :] for s in range(half)]
            sums = [a + b for a, b in zip(low, high)]
            diffs = [a - b for a, b in zip(low, high)]
            for t in range(half):
                acc, dif = None, None
                for s in range(half):
                    if abs(plus[t, s]) > 1e-12:
                        term = sums[s] * float(plus[t, s])
                        acc = term if acc is None else acc + term
                    if abs(minus[t, s]) > 1e-12:
                        term = diffs[s] * float(minus[t, s])
                        dif = term if dif is None else dif + term
                ybuf[sweep, t, at, :] = acc + dif
                ybuf[sweep, t + half, at, :] = acc - dif
            return 0
        lax.fori_loop(0, size // 8, group, 0)

    src_row = lax.broadcasted_iota(jnp.int32, (LANES, LANES), 0)
    dst_col = lax.broadcasted_iota(jnp.int32, (LANES, LANES), 1)

    def onehot(mask):
        return jnp.where(mask, 1.0, 0.0).astype(F32)

    def build_weights():
        lane_var = lax.broadcasted_iota(jnp.int32, (1, block), 1) // 64
        tiles = [jnp.concatenate([nodes[i]] * width, axis=1) for i in range(10)]
        for w in range(width):
            fe = []
            for d in range(3):
                row = jnp.zeros((1, block), F32)
                for v in range(width):
                    row = jnp.where(lane_var == v, flux[w, d:d + 1, v:v + 1], row)
                fe.append(row)
            same = jnp.where(lane_var == w, 1.0, 0.0)
            parts = [fe[0] * tiles[0] + fe[1] * tiles[1] + fe[2] * tiles[2] + same * tiles[3]]
            for d in range(3):
                parts.append(fe[d] * tiles[4 + 2 * d] + same * tiles[5 + 2 * d])
            hi, lo = split(jnp.concatenate(parts, axis=1))
            wh[w * 64:(w + 1) * 64, :] = hi
            wl[w * 64:(w + 1) * 64, :] = lo

    def build_moves():
        layer = (lax.broadcasted_iota(jnp.int32, (1, LANES), 1) // cells) * cells
        for f in range(4):
            nb = cross[f:f + 1, :]
            nb = jnp.concatenate([nb] * (LANES // cells), axis=1) + layer
            ref = py if f < 2 else pz
            ref[(f % 2) * LANES:(f % 2 + 1) * LANES, :] = onehot(src_row == nb).astype(BF)

    def build_match():
        last = LANES - cells
        low_ok = jnp.where(sp > 0, 1.0, 0.0)
        high_ok = jnp.where(sp < ns - 1, 1.0, 0.0)
        shift_up = onehot(dst_col == src_row + cells).astype(BF)
        shift_down = onehot(src_row == dst_col + cells).astype(BF)
        for t in range(T):
            m = jnp.concatenate([match[t]] * (LANES // cells), axis=1)
            mu = jnp.concatenate([match_up[t]] * (LANES // cells), axis=1)
            pb[t, 0:LANES, :] = shift_up
            pb[t, LANES:, :] = (onehot((dst_col < cells) & (src_row == m + last)) * low_ok).astype(BF)
            pa[t, 0:LANES, :] = shift_down
            turned = onehot((dst_col < cells) & (src_row == mu + last)) * high_ok
            pa[t, LANES:, :] = turned.T.astype(BF)

    row_id = lax.broadcasted_iota(jnp.int32, (block, 1), 0)

    def as_mask(index, value):
        return jnp.where(index == value, 1.0, 0.0).astype(F32)

    mj3, mj0 = as_mask((row_id >> 2) & 3, 3), as_mask((row_id >> 2) & 3, 0)
    mk3, mk0 = as_mask(row_id & 3, 3), as_mask(row_id & 3, 0)

    def spread_cross(src, t):
        cols = slice(t * LANES, (t + 1) * LANES)
        x = src[t, 0:block, :]
        for part, out in zip(split(x), (vh, vl)):
            out[0:block, cols] = part
            wide = part.astype(F32)
            y = jnp.concatenate([wide * mj3, wide * mj0], axis=1).astype(BF)
            z = jnp.concatenate([wide * mk3, wide * mk0], axis=1).astype(BF)
            out[2 * block:3 * block, cols] = mm(y, py[...]).astype(BF)
            out[3 * block:4 * block, cols] = mm(z, pz[...]).astype(BF)

    def spread_flow(sweep, src, t):
        cols = slice(t * LANES, (t + 1) * LANES)
        own_high = jnp.concatenate([src[t, v * 64 + 48:v * 64 + 64, :] for v in range(width)], axis=0)
        own_low = jnp.concatenate([src[t, v * 64:v * 64 + 16, :] for v in range(width)], axis=0)
        high = split(jnp.concatenate([own_high, halo[sweep, 0, t]], axis=1))
        low = split(jnp.concatenate([own_low, halo[sweep, 1, t]], axis=1))
        for i, out in enumerate((vh, vl)):
            ub = mm(high[i], pb[t]).astype(BF)
            ua = mm(low[i], pa[t]).astype(BF)
            for v in range(width):
                base = block + v * 64
                out[base:base + 16, cols] = ua[v * 16:(v + 1) * 16]
                out[base + 48:base + 64, cols] = ub[v * 16:(v + 1) * 16]

    def clear_middle():
        for out in (vh, vl):
            for v in range(width):
                base = block + v * 64 + 16
                out[base:base + 32, :] = jnp.zeros((32, T * LANES), BF)

    def split_jac():
        load_j.wait()
        place = lax.broadcasted_iota(jnp.int32, (block, block), 0)
        column = lax.broadcasted_iota(jnp.int32, (block, block), 1)
        chosen, at = column < 0, 0
        for start, size in first + second:
            chosen = chosen | ((column >= at) & (column < at + size) & (place - column == start - at))
            at += size
        chosen = onehot(chosen).astype(BF)
        for t in range(T):
            hi, lo = [mm(part, chosen).astype(BF) for part in split(jac[t])]
            jone[t] = jnp.concatenate([hi[:, :early], lo[:, :early], hi[:, :early]], axis=1)
            jtwo[t] = jnp.concatenate([hi[:, early:], lo[:, early:], hi[:, early:]], axis=1)

    def apply_space(spat):
        total = mm(wh[...], vh[...]) + mm(wl[...], vh[...]) + mm(wh[...], vl[...])
        for t in range(T):
            spat[t] = total[:, t * LANES:(t + 1) * LANES] - forc[t]

    lead, held, near = range(quarter), range(quarter, side), range(side, n - 1)

    def start_early(sweep):
        if sweep == 0:
            for k in everyone:
                backward(k, T).start()
            return
        for g in range(len(groups)):
            for k in (*lead, *near):
                backward_last(k, 0, g).start()

    def start_late(sweep):
        if sweep == 0:
            for c in range(T):
                for k in everyone:
                    backward(k, c).start()
            return
        for g in range(len(groups)):
            for k in lead:
                backward_last(k, 1, g).start()
        for g in range(len(groups)):
            for k in near:
                backward_last(k, 1, g).start()
        for g in range(len(groups)):
            for part in range(2):
                for k in held:
                    backward_last(k, part, g).start()

    own_rows = pl.ds(pl.multiple_of(me * rows, 8), rows)
    own_times = pl.ds(me * T, T)

    def run_sweep(sweep, src, before, between):
        xbuf[sweep, own_times, :, :] = src[:, own_rows, :]
        for job in before:
            job()
        wait_forward(sweep, 0)
        derive(sweep, 0, arows)
        start_early(sweep)
        for job in between:
            job()
        wait_forward(sweep, 1)
        derive(sweep, arows, brows)
        start_late(sweep)
        dbuf[sweep, :, own_rows, :] = ybuf[sweep, own_times, :, :]

    def step(sweep, spat, t, spans, weights):
        r = []
        for start, size in spans:
            at = slice(start, start + size)
            r.append(spat[t, at, :] + dbuf[sweep, t, at, :])
            if sweep == 0:
                spat[t, at, :] = r[-1]
        hi, lo = split(jnp.concatenate(r, axis=0))
        return mm(weights[t], jnp.concatenate([hi, hi, lo], axis=0))

    def finish(src, spat, dst, after):
        wait_backward(T)
        for t in range(T):
            part[t] = src[t, 0:block, :] - step(0, spat, t, first, jone)
        for t in range(T):
            wait_backward(t)
            dst[t, 0:block, :] = part[t] - step(0, spat, t, second, jtwo)
            after(t)

    def finish_last(src, spat, dst):
        for g, (t0, nt) in enumerate(groups):
            wait_last(g, 0)
            for t in range(t0, t0 + nt):
                part[t] = src[t, 0:block, :] - step(1, spat, t, first, jone)
            wait_last(g, 1)
            for t in range(t0, t0 + nt):
                dst[t, 0:block, :] = part[t] - step(1, spat, t, second, jtwo)

    def send_forward(sweep, src, c):
        for k in everyone:
            forward(sweep, src, k, c).start()

    def wait_halos(sweep, src):
        drain(halo.at[sweep], hrecv.at[sweep])

    def first_halo_ready():
        send_match.wait()
        wait_halos(0, state)
        build_match()

    for c in (0, T):
        send_forward(0, exact0, c)
    for load in loads[2:]:
        load.start()
    send_match.start()
    for h in halos(0, state):
        h.start()
    before = [load_c.wait, build_moves, load_n.wait, load_x.wait, build_weights]
    before += [functools.partial(spread_cross, state, t) for t in range(T)]
    before += [clear_middle]
    between = [first_halo_ready]
    between += [functools.partial(spread_flow, 0, state, t) for t in range(T)]
    between += [load_f.wait, functools.partial(apply_space, res), split_jac]
    run_sweep(0, exact0, before, between)
    cur = v1.at[1]
    finish(state, res, cur, lambda t: send_forward(1, cur, t))

    send_forward(1, cur, T)
    for h in halos(1, cur):
        h.start()
    before = [functools.partial(spread_cross, cur, t) for t in range(T)]
    between = [functools.partial(wait_halos, 1, cur)]
    between += [functools.partial(spread_flow, 1, cur, t) for t in range(T)]
    between += [functools.partial(apply_space, spat1)]
    run_sweep(1, cur, before, between)
    finish_last(cur, spat1, upd)
    drain(xbuf.at[:, others, :, :], send_sem.at[0])
    drain(ybuf.at[:, others, :, :], send_sem.at[1])
    drain(halo, send_sem.at[2])


def hand_out(res_vmem, upd_vmem, res_hbm, upd_hbm, sem):
    copies = [
        pltpu.make_async_copy(res_vmem, res_hbm, sem.at[0]),
        pltpu.make_async_copy(upd_vmem, upd_hbm, sem.at[1]),
    ]
    for copy in copies:
        copy.start()
    for copy in copies:
        copy.wait()


def body(n, ns, state, forcing, flux_jac, jacobi_inv, cross_nbr, lower_match):
    T, block, elements = state.shape
    width = flux_jac.shape[1]
    cells = cross_nbr.shape[1]
    count = n * T
    rows = -(-block // (8 * n)) * 8
    arows = -(-rows // 16) * 8
    halo_rows = width * 16
    early = sum(max(0, min(arows, block - p * rows)) for p in range(n))
    flux = flux_jac.transpose(1, 0, 2)
    nodes = jnp.asarray(node_matrices())
    cfg = (n, ns, T, width, rows, arows, count, cells)
    full = n * rows
    dma = pltpu.SemaphoreType.DMA
    vmem = pl.BlockSpec(memory_space=pltpu.VMEM)
    hbm = pl.BlockSpec(memory_space=pl.ANY)
    held = pltpu.VMEM(state.shape, F32)
    res, upd = pl.pallas_call(
        functools.partial(kernel, cfg),
        name="sweeps",
        out_shape=(held, held),
        in_specs=[hbm] * 7,
        out_specs=(vmem, vmem),
        scratch_shapes=[
            pltpu.VMEM((SWEEPS, count, rows, LANES), F32),
            pltpu.VMEM((SWEEPS, count, rows, LANES), F32),
            pltpu.VMEM((SWEEPS, T, full, LANES), F32),
            pltpu.VMEM((SWEEPS, 2, T, halo_rows, LANES), F32),
            pltpu.VMEM((T, 1, cells), jnp.int32),
            pltpu.VMEM((2, T, full, LANES), F32),
            pltpu.VMEM((T, block, LANES), F32),
            pltpu.VMEM((T, block, LANES), F32),
            pltpu.VMEM((T, block, LANES), F32),
            pltpu.VMEM((T, block, block), F32),
            pltpu.VMEM((T, block, 3 * early), BF),
            pltpu.VMEM((T, block, 3 * (block - early)), BF),
            pltpu.VMEM((4 * block, T * LANES), BF),
            pltpu.VMEM((4 * block, T * LANES), BF),
            pltpu.VMEM((block, 4 * block), BF),
            pltpu.VMEM((block, 4 * block), BF),
            pltpu.VMEM((2 * LANES, LANES), BF),
            pltpu.VMEM((2 * LANES, LANES), BF),
            pltpu.VMEM((T, 2 * LANES, LANES), BF),
            pltpu.VMEM((T, 2 * LANES, LANES), BF),
            pltpu.VMEM(flux.shape, F32),
            pltpu.VMEM(nodes.shape, F32),
            pltpu.VMEM(cross_nbr.shape, jnp.int32),
            pltpu.VMEM(lower_match.shape, jnp.int32),
            pltpu.VMEM((T, block, LANES), F32),
            dma((3,)),
            dma((2,)),
            dma((T + 1,)),
            dma((SWEEPS,)),
            dma((2,)),
            dma((5,)),
        ],
        compiler_params=pltpu.CompilerParams(
            collective_id=0, has_side_effects=True, vmem_limit_bytes=56 * 1024 * 1024
        ),
    )(flux, nodes, cross_nbr, lower_match, state, forcing, jacobi_inv)
    out = jax.ShapeDtypeStruct(state.shape, F32)
    return pl.pallas_call(
        hand_out,
        name="hand_out",
        out_shape=(out, out),
        in_specs=[vmem] * 2,
        out_specs=(hbm, hbm),
        scratch_shapes=[dma((2,))],
    )(pltpu.with_memory_space_constraint(res, pltpu.VMEM), pltpu.with_memory_space_constraint(upd, pltpu.VMEM))


def solution(mesh):
    n, ns = mesh.shape["inst"], mesh.shape["space"]
    return jax.shard_map(
        functools.partial(body, n, ns),
        mesh=mesh,
        in_specs=(
            P("inst", None, "space"),
            P("inst", None, "space"),
            P(),
            P("inst", None, None),
            P(),
            P("inst", "space", None),
        ),
        out_specs=(P("inst", None, "space"), P("inst", None, "space")),
        check_vma=False,
    )
```

```python
import functools
import math

import jax
import jax.numpy as jnp
import numpy as np
from jax import lax
from jax.experimental import pallas as pl
from jax.experimental.pallas import tpu as pltpu
from jax.sharding import PartitionSpec as P

NODE1 = 4
SWEEPS = 2
DISSIPATION = 0.6
FREQUENCY = 0.25
LANES = 128
MESH = pl.DeviceIdType.MESH
BF = jnp.bfloat16
F32 = jnp.float32


def lobatto_derivative(count_of_nodes):
    inner_point = math.sqrt(0.2)
    points = np.array([-1.0, -inner_point, inner_point, 1.0])
    bary = np.ones(count_of_nodes)
    for a in range(count_of_nodes):
        for b in range(count_of_nodes):
            if a != b:
                bary[a] = bary[a] / (points[a] - points[b])
    table = np.zeros((count_of_nodes, count_of_nodes))
    for a in range(count_of_nodes):
        for b in range(count_of_nodes):
            if a != b:
                table[a, b] = bary[b] / bary[a] / (points[a] - points[b])
        table[a, a] = -np.sum(table[a])
    return table


def node_matrices():
    n = NODE1
    scale = n * (n - 1) / 4.0
    der = lobatto_derivative(n).astype(np.float32).astype(np.float64)
    eye = np.eye(n)
    low, high = np.zeros((n, n)), np.zeros((n, n))
    low[0, 0] = 1.0
    high[n - 1, n - 1] = 1.0
    to_low, to_high = np.zeros((n, n)), np.zeros((n, n))
    to_low[0, n - 1] = 1.0
    to_high[n - 1, 0] = 1.0

    def place(m, d):
        parts = [eye, eye, eye]
        parts[d] = m
        return np.kron(np.kron(parts[0], parts[1]), parts[2])

    own = [place(der + scale * (low - high), d) for d in range(3)]
    own.append(DISSIPATION * scale * sum(place(low + high, d) for d in range(3)))
    for d in range(3):
        own.append(place(scale * (to_high - to_low), d))
        own.append(-DISSIPATION * scale * place(to_high + to_low, d))
    return np.stack(own).astype(np.float32)


def time_weights(count):
    half = count // 2
    d = np.zeros(count)
    for m in range(1, count):
        d[m] = 0.5 * FREQUENCY * (-1.0) ** m / math.tan(math.pi * m / count)
    d[half] = 0.0
    plus = np.zeros((half, half))
    minus = np.zeros((half, half))
    for t in range(half):
        for s in range(half):
            a, b = d[(t - s) % count], d[(t - s + half) % count]
            plus[t, s] = 0.5 * (a + b)
            minus[t, s] = 0.5 * (a - b)
    return plus, minus


def split(x):
    hi = x.astype(BF)
    return hi, (x - hi.astype(F32)).astype(BF)


def mm(a, b):
    return jnp.dot(a, b, preferred_element_type=F32)


def kernel(
    cfg, flux_hbm, nodes_hbm, cross_hbm, match_hbm, state_hbm, forcing_hbm, jac_hbm, res, upd,
    xbuf, ybuf, dbuf, halo, match_up, v1, spat1, part, forc, jac, jone, jtwo, vh, vl, wh, wl, py, pz, pb, pa,
    flux, nodes, cross, match, state, send_sem, frecv, brecv, hrecv, mrecv, lsem,
):
    n, ns, T, width, rows, arows, count, cells = cfg
    brows = rows - arows
    block = width * 64
    first = [(p * rows, min(arows, block - p * rows)) for p in range(n) if p * rows < block]
    second = [(p * rows + arows, min(brows, block - p * rows - arows)) for p in range(n) if p * rows + arows < block]
    early = sum(size for _, size in first)
    me = lax.axis_index("inst")
    sp = lax.axis_index("space")
    right, left = lax.rem(sp + 1, ns), lax.rem(sp + ns - 1, ns)
    side, quarter = n // 2, n // 4
    high = jnp.where(me >= side, 1, 0)
    own, other = high * side, (1 - high) * side
    inner, odd = me - own, me % 2
    ranked = [other + lax.rem(k + (1 - high) * quarter, side) for k in range(side)]
    peers = [other + lax.rem(k + odd * (1 - 2 * (k % 2)) + (1 - high) * quarter, side) for k in range(side)]
    peers += [own + lax.rem(inner + k, side) for k in (*range(quarter, side), *range(1, quarter))]

    barrier = pltpu.get_barrier_semaphore()
    for p in peers:
        pl.semaphore_signal(barrier, inc=1, device_id={"inst": p}, device_id_type=MESH)
    for p in (right, left):
        pl.semaphore_signal(barrier, inc=1, device_id={"space": p}, device_id_type=MESH)

    pairs = (
        (state_hbm, state), (match_hbm, match), (cross_hbm, cross), (flux_hbm, flux),
        (nodes_hbm, nodes), (forcing_hbm, forc), (jac_hbm, jac),
    )
    loads = [pltpu.make_async_copy(a, b, lsem.at[i % 5]) for i, (a, b) in enumerate(pairs)]
    load_s, load_m, load_c, load_x, load_n, load_f, load_j = loads
    load_s.start()
    load_m.start()
    load_s.wait()
    load_m.wait()
    pl.semaphore_wait(barrier, n + 1)

    padded = n * rows != block
    exact0 = state
    if padded:
        for t in range(T):
            v1[0, t, 0:block, :] = state[t]
            v1[0, t, block:, :] = jnp.zeros((n * rows - block, LANES), F32)
            v1[1, t, block:, :] = jnp.zeros((n * rows - block, LANES), F32)
        exact0 = v1.at[0]

    def forward(sweep, src, k, c):
        p = peers[k]
        if sweep == 0 and c == 0:
            t0, nt, r0, nr = 0, T, 0, arows
        elif c < T:
            t0, nt, r0, nr = c, 1, 0, arows
        else:
            t0, nt, r0, nr = 0, T, arows, brows
        return pltpu.make_async_remote_copy(
            src_ref=src.at[pl.ds(t0, nt), pl.ds(pl.multiple_of(p * rows + r0, 8), nr), :],
            dst_ref=xbuf.at[sweep, pl.ds(me * T + t0, nt), pl.ds(r0, nr), :],
            send_sem=send_sem.at[0],
            recv_sem=frecv.at[c // T],
            device_id={"inst": p},
            device_id_type=MESH,
        )

    def piece(sweep, k, part, t0, nt, sem):
        p = ranked[k] if sweep > 0 and k < side else peers[k]
        r0, nr = ((0, arows), (arows, brows))[part]
        return pltpu.make_async_remote_copy(
            src_ref=ybuf.at[sweep, pl.ds(p * T + t0, nt), pl.ds(r0, nr), :],
            dst_ref=dbuf.at[sweep, pl.ds(t0, nt), pl.ds(pl.multiple_of(me * rows + r0, 8), nr), :],
            send_sem=send_sem.at[1],
            recv_sem=brecv.at[sem],
            device_id={"inst": p},
            device_id_type=MESH,
        )

    def backward(k, c):
        if c < T:
            return piece(0, k, 1, c, 1, c)
        return piece(0, k, 0, 0, T, T)

    def backward_last(k, part, g):
        t0, nt = groups[g]
        return piece(SWEEPS - 1, k, part, t0, nt, 2 * g + part)

    everyone = range(n - 1)
    groups = [(t0, min(2, T - t0)) for t0 in range(0, T, 2)]
    others = pl.ds(0, (n - 1) * T)

    def drain(view, sem):
        pltpu.make_async_copy(view, view, sem).wait()

    def wait_forward(sweep, part):
        at = pl.ds(arows, brows) if part else pl.ds(0, arows)
        drain(xbuf.at[sweep, others, at, :], frecv.at[part])

    def wait_backward(c):
        if c == T:
            drain(dbuf.at[0, :, pl.ds(0, (n - 1) * arows), :], brecv.at[T])
        else:
            drain(dbuf.at[0, c, pl.ds(0, (n - 1) * brows), :], brecv.at[c])

    def wait_last(g, part):
        t0, nt = groups[g]
        size = (n - 1) * (arows, brows)[part]
        drain(dbuf.at[SWEEPS - 1, pl.ds(t0, nt), pl.ds(0, size), :], brecv.at[2 * g + part])

    def halos(sweep, src):
        out = []
        for t in range(T):
            for v in range(width):
                up = v * 64 + 48
                down = v * 64
                out.append(pltpu.make_async_remote_copy(
                    src_ref=src.at[t, pl.ds(up, 16), :],
                    dst_ref=halo.at[sweep, 0, t, pl.ds(v * 16, 16), :],
                    send_sem=send_sem.at[2],
                    recv_sem=hrecv.at[sweep],
                    device_id={"space": right}, device_id_type=MESH))
                out.append(pltpu.make_async_remote_copy(
                    src_ref=src.at[t, pl.ds(down, 16), :],
                    dst_ref=halo.at[sweep, 1, t, pl.ds(v * 16, 16), :],
                    send_sem=send_sem.at[2],
                    recv_sem=hrecv.at[sweep],
                    device_id={"space": left}, device_id_type=MESH))
        return out

    send_match = pltpu.make_async_remote_copy(
        src_ref=match, dst_ref=match_up, send_sem=mrecv.at[0], recv_sem=mrecv.at[1],
        device_id={"space": left}, device_id_type=MESH)

    plus, minus = time_weights(count)
    half = count // 2

    def derive(sweep, first, size):
        def group(g, _):
            at = pl.ds(pl.multiple_of(first + g * 8, 8), 8)
            low = [xbuf[sweep, s, at, :] for s in range(half)]
            high = [xbuf[sweep, s + half, at, :] for s in range(half)]
            sums = [a + b for a, b in zip(low, high)]
            diffs = [a - b for a, b in zip(low, high)]
            for t in range(half):
                acc, dif = None, None
                for s in range(half):
                    if abs(plus[t, s]) > 1e-12:
                        term = sums[s] * float(plus[t, s])
                        acc = term if acc is None else acc + term
                    if abs(minus[t, s]) > 1e-12:
                        term = diffs[s] * float(minus[t, s])
                        dif = term if dif is None else dif + term
                ybuf[sweep, t, at, :] = acc + dif
                ybuf[sweep, t + half, at, :] = acc - dif
            return 0
        lax.fori_loop(0, size // 8, group, 0)

    src_row = lax.broadcasted_iota(jnp.int32, (LANES, LANES), 0)
    dst_col = lax.broadcasted_iota(jnp.int32, (LANES, LANES), 1)

    def onehot(mask):
        return jnp.where(mask, 1.0, 0.0).astype(F32)

    def build_weights():
        lane_var = lax.broadcasted_iota(jnp.int32, (1, block), 1) // 64
        tiles = [jnp.concatenate([nodes[i]] * width, axis=1) for i in range(10)]
        for w in range(width):
            fe = []
            for d in range(3):
                row = jnp.zeros((1, block), F32)
                for v in range(width):
                    row = jnp.where(lane_var == v, flux[w, d:d + 1, v:v + 1], row)
                fe.append(row)
            same = jnp.where(lane_var == w, 1.0, 0.0)
            parts = [fe[0] * tiles[0] + fe[1] * tiles[1] + fe[2] * tiles[2] + same * tiles[3]]
            for d in range(3):
                parts.append(fe[d] * tiles[4 + 2 * d] + same * tiles[5 + 2 * d])
            hi, lo = split(jnp.concatenate(parts, axis=1))
            wh[w * 64:(w + 1) * 64, :] = hi
            wl[w * 64:(w + 1) * 64, :] = lo

    def build_moves():
        layer = (lax.broadcasted_iota(jnp.int32, (1, LANES), 1) // cells) * cells
        for f in range(4):
            nb = cross[f:f + 1, :]
            nb = jnp.concatenate([nb] * (LANES // cells), axis=1) + layer
            ref = py if f < 2 else pz
            ref[(f % 2) * LANES:(f % 2 + 1) * LANES, :] = onehot(src_row == nb).astype(BF)

    def build_match():
        last = LANES - cells
        low_ok = jnp.where(sp > 0, 1.0, 0.0)
        high_ok = jnp.where(sp < ns - 1, 1.0, 0.0)
        shift_up = onehot(dst_col == src_row + cells).astype(BF)
        shift_down = onehot(src_row == dst_col + cells).astype(BF)
        for t in range(T):
            m = jnp.concatenate([match[t]] * (LANES // cells), axis=1)
            mu = jnp.concatenate([match_up[t]] * (LANES // cells), axis=1)
            pb[t, 0:LANES, :] = shift_up
            pb[t, LANES:, :] = (onehot((dst_col < cells) & (src_row == m + last)) * low_ok).astype(BF)
            pa[t, 0:LANES, :] = shift_down
            turned = onehot((dst_col < cells) & (src_row == mu + last)) * high_ok
            pa[t, LANES:, :] = turned.T.astype(BF)

    row_id = lax.broadcasted_iota(jnp.int32, (block, 1), 0)

    def as_mask(index, value):
        return jnp.where(index == value, 1.0, 0.0).astype(F32)

    mj3, mj0 = as_mask((row_id >> 2) & 3, 3), as_mask((row_id >> 2) & 3, 0)
    mk3, mk0 = as_mask(row_id & 3, 3), as_mask(row_id & 3, 0)

    def spread_cross(src, t):
        cols = slice(t * LANES, (t + 1) * LANES)
        x = src[t, 0:block, :]
        for part, out in zip(split(x), (vh, vl)):
            out[0:block, cols] = part
            wide = part.astype(F32)
            y = jnp.concatenate([wide * mj3, wide * mj0], axis=1).astype(BF)
            z = jnp.concatenate([wide * mk3, wide * mk0], axis=1).astype(BF)
            out[2 * block:3 * block, cols] = mm(y, py[...]).astype(BF)
            out[3 * block:4 * block, cols] = mm(z, pz[...]).astype(BF)

    def spread_flow(sweep, src, t):
        cols = slice(t * LANES, (t + 1) * LANES)
        own_high = jnp.concatenate([src[t, v * 64 + 48:v * 64 + 64, :] for v in range(width)], axis=0)
        own_low = jnp.concatenate([src[t, v * 64:v * 64 + 16, :] for v in range(width)], axis=0)
        high = split(jnp.concatenate([own_high, halo[sweep, 0, t]], axis=1))
        low = split(jnp.concatenate([own_low, halo[sweep, 1, t]], axis=1))
        for i, out in enumerate((vh, vl)):
            ub = mm(high[i], pb[t]).astype(BF)
            ua = mm(low[i], pa[t]).astype(BF)
            for v in range(width):
                base = block + v * 64
                out[base:base + 16, cols] = ua[v * 16:(v + 1) * 16]
                out[base + 48:base + 64, cols] = ub[v * 16:(v + 1) * 16]

    def clear_middle():
        for out in (vh, vl):
            for v in range(width):
                base = block + v * 64 + 16
                out[base:base + 32, :] = jnp.zeros((32, T * LANES), BF)

    def split_jac():
        load_j.wait()
        place = lax.broadcasted_iota(jnp.int32, (block, block), 0)
        column = lax.broadcasted_iota(jnp.int32, (block, block), 1)
        chosen, at = column < 0, 0
        for start, size in first + second:
            chosen = chosen | ((column >= at) & (column < at + size) & (place - column == start - at))
            at += size
        chosen = onehot(chosen).astype(BF)
        for t in range(T):
            hi, lo = [mm(part, chosen).astype(BF) for part in split(jac[t])]
            jone[t] = jnp.concatenate([hi[:, :early], lo[:, :early], hi[:, :early]], axis=1)
            jtwo[t] = jnp.concatenate([hi[:, early:], lo[:, early:], hi[:, early:]], axis=1)

    def apply_space(spat):
        total = mm(wh[...], vh[...]) + mm(wl[...], vh[...]) + mm(wh[...], vl[...])
        for t in range(T):
            spat[t] = total[:, t * LANES:(t + 1) * LANES] - forc[t]

    lead, held, near = range(quarter), range(quarter, side), range(side, n - 1)

    def start_early(sweep):
        if sweep == 0:
            for k in everyone:
                backward(k, T).start()
            return
        for g in range(len(groups)):
            for k in (*lead, *near):
                backward_last(k, 0, g).start()

    def start_late(sweep):
        if sweep == 0:
            for c in range(T):
                for k in everyone:
                    backward(k, c).start()
            return
        for g in range(len(groups)):
            for k in lead:
                backward_last(k, 1, g).start()
        for g in range(len(groups)):
            for k in near:
                backward_last(k, 1, g).start()
        for k in held:
            for g in range(len(groups)):
                for part in range(2):
                    backward_last(k, part, g).start()

    own_rows = pl.ds(pl.multiple_of(me * rows, 8), rows)
    own_times = pl.ds(me * T, T)

    def run_sweep(sweep, src, before, between):
        xbuf[sweep, own_times, :, :] = src[:, own_rows, :]
        for job in before:
            job()
        wait_forward(sweep, 0)
        derive(sweep, 0, arows)
        start_early(sweep)
        for job in between:
            job()
        wait_forward(sweep, 1)
        derive(sweep, arows, brows)
        start_late(sweep)
        dbuf[sweep, :, own_rows, :] = ybuf[sweep, own_times, :, :]

    def step(sweep, spat, t, spans, weights):
        r = []
        for start, size in spans:
            at = slice(start, start + size)
            r.append(spat[t, at, :] + dbuf[sweep, t, at, :])
            if sweep == 0:
                spat[t, at, :] = r[-1]
        hi, lo = split(jnp.concatenate(r, axis=0))
        return mm(weights[t], jnp.concatenate([hi, hi, lo], axis=0))

    def finish(src, spat, dst, after):
        wait_backward(T)
        for t in range(T):
            part[t] = src[t, 0:block, :] - step(0, spat, t, first, jone)
        for t in range(T):
            wait_backward(t)
            dst[t, 0:block, :] = part[t] - step(0, spat, t, second, jtwo)
            after(t)

    def finish_last(src, spat, dst):
        for g, (t0, nt) in enumerate(groups):
            wait_last(g, 0)
            for t in range(t0, t0 + nt):
                part[t] = src[t, 0:block, :] - step(1, spat, t, first, jone)
            wait_last(g, 1)
            for t in range(t0, t0 + nt):
                dst[t, 0:block, :] = part[t] - step(1, spat, t, second, jtwo)

    def send_forward(sweep, src, c):
        for k in everyone:
            forward(sweep, src, k, c).start()

    def wait_halos(sweep, src):
        drain(halo.at[sweep], hrecv.at[sweep])

    def first_halo_ready():
        send_match.wait()
        wait_halos(0, state)
        build_match()

    for c in (0, T):
        send_forward(0, exact0, c)
    for load in loads[2:]:
        load.start()
    send_match.start()
    for h in halos(0, state):
        h.start()
    before = [load_c.wait, build_moves, load_n.wait, load_x.wait, build_weights]
    before += [functools.partial(spread_cross, state, t) for t in range(T)]
    before += [clear_middle]
    between = [first_halo_ready]
    between += [functools.partial(spread_flow, 0, state, t) for t in range(T)]
    between += [load_f.wait, functools.partial(apply_space, res), split_jac]
    run_sweep(0, exact0, before, between)
    cur = v1.at[1]
    finish(state, res, cur, lambda t: send_forward(1, cur, t))

    send_forward(1, cur, T)
    for h in halos(1, cur):
        h.start()
    before = [functools.partial(spread_cross, cur, t) for t in range(T)]
    between = [functools.partial(wait_halos, 1, cur)]
    between += [functools.partial(spread_flow, 1, cur, t) for t in range(T)]
    between += [functools.partial(apply_space, spat1)]
    run_sweep(1, cur, before, between)
    finish_last(cur, spat1, upd)
    drain(xbuf.at[:, others, :, :], send_sem.at[0])
    drain(ybuf.at[:, others, :, :], send_sem.at[1])
    drain(halo, send_sem.at[2])


def hand_out(res_vmem, upd_vmem, res_hbm, upd_hbm, sem):
    copies = [
        pltpu.make_async_copy(res_vmem, res_hbm, sem.at[0]),
        pltpu.make_async_copy(upd_vmem, upd_hbm, sem.at[1]),
    ]
    for copy in copies:
        copy.start()
    for copy in copies:
        copy.wait()


def body(n, ns, state, forcing, flux_jac, jacobi_inv, cross_nbr, lower_match):
    T, block, elements = state.shape
    width = flux_jac.shape[1]
    cells = cross_nbr.shape[1]
    count = n * T
    rows = -(-block // (8 * n)) * 8
    arows = -(-rows // 16) * 8
    halo_rows = width * 16
    early = sum(max(0, min(arows, block - p * rows)) for p in range(n))
    flux = flux_jac.transpose(1, 0, 2)
    nodes = jnp.asarray(node_matrices())
    cfg = (n, ns, T, width, rows, arows, count, cells)
    full = n * rows
    dma = pltpu.SemaphoreType.DMA
    vmem = pl.BlockSpec(memory_space=pltpu.VMEM)
    hbm = pl.BlockSpec(memory_space=pl.ANY)
    held = pltpu.VMEM(state.shape, F32)
    res, upd = pl.pallas_call(
        functools.partial(kernel, cfg),
        name="sweeps",
        out_shape=(held, held),
        in_specs=[hbm] * 7,
        out_specs=(vmem, vmem),
        scratch_shapes=[
            pltpu.VMEM((SWEEPS, count, rows, LANES), F32),
            pltpu.VMEM((SWEEPS, count, rows, LANES), F32),
            pltpu.VMEM((SWEEPS, T, full, LANES), F32),
            pltpu.VMEM((SWEEPS, 2, T, halo_rows, LANES), F32),
            pltpu.VMEM((T, 1, cells), jnp.int32),
            pltpu.VMEM((2, T, full, LANES), F32),
            pltpu.VMEM((T, block, LANES), F32),
            pltpu.VMEM((T, block, LANES), F32),
            pltpu.VMEM((T, block, LANES), F32),
            pltpu.VMEM((T, block, block), F32),
            pltpu.VMEM((T, block, 3 * early), BF),
            pltpu.VMEM((T, block, 3 * (block - early)), BF),
            pltpu.VMEM((4 * block, T * LANES), BF),
            pltpu.VMEM((4 * block, T * LANES), BF),
            pltpu.VMEM((block, 4 * block), BF),
            pltpu.VMEM((block, 4 * block), BF),
            pltpu.VMEM((2 * LANES, LANES), BF),
            pltpu.VMEM((2 * LANES, LANES), BF),
            pltpu.VMEM((T, 2 * LANES, LANES), BF),
            pltpu.VMEM((T, 2 * LANES, LANES), BF),
            pltpu.VMEM(flux.shape, F32),
            pltpu.VMEM(nodes.shape, F32),
            pltpu.VMEM(cross_nbr.shape, jnp.int32),
            pltpu.VMEM(lower_match.shape, jnp.int32),
            pltpu.VMEM((T, block, LANES), F32),
            dma((3,)),
            dma((2,)),
            dma((T + 1,)),
            dma((SWEEPS,)),
            dma((2,)),
            dma((5,)),
        ],
        compiler_params=pltpu.CompilerParams(
            collective_id=0, has_side_effects=True, vmem_limit_bytes=56 * 1024 * 1024
        ),
    )(flux, nodes, cross_nbr, lower_match, state, forcing, jacobi_inv)
    out = jax.ShapeDtypeStruct(state.shape, F32)
    return pl.pallas_call(
        hand_out,
        name="hand_out",
        out_shape=(out, out),
        in_specs=[vmem] * 2,
        out_specs=(hbm, hbm),
        scratch_shapes=[dma((2,))],
    )(pltpu.with_memory_space_constraint(res, pltpu.VMEM), pltpu.with_memory_space_constraint(upd, pltpu.VMEM))


def solution(mesh):
    n, ns = mesh.shape["inst"], mesh.shape["space"]
    return jax.shard_map(
        functools.partial(body, n, ns),
        mesh=mesh,
        in_specs=(
            P("inst", None, "space"),
            P("inst", None, "space"),
            P(),
            P("inst", None, None),
            P(),
            P("inst", "space", None),
        ),
        out_specs=(P("inst", None, "space"), P("inst", None, "space")),
        check_vma=False,
    )
```

```python
import functools
import math

import jax
import jax.numpy as jnp
import numpy as np
from jax import lax
from jax.experimental import pallas as pl
from jax.experimental.pallas import tpu as pltpu
from jax.sharding import PartitionSpec as P

NODE1 = 4
SWEEPS = 2
DISSIPATION = 0.6
FREQUENCY = 0.25
LANES = 128
MESH = pl.DeviceIdType.MESH
BF = jnp.bfloat16
F32 = jnp.float32


def lobatto_derivative(count_of_nodes):
    inner_point = math.sqrt(0.2)
    points = np.array([-1.0, -inner_point, inner_point, 1.0])
    bary = np.ones(count_of_nodes)
    for a in range(count_of_nodes):
        for b in range(count_of_nodes):
            if a != b:
                bary[a] = bary[a] / (points[a] - points[b])
    table = np.zeros((count_of_nodes, count_of_nodes))
    for a in range(count_of_nodes):
        for b in range(count_of_nodes):
            if a != b:
                table[a, b] = bary[b] / bary[a] / (points[a] - points[b])
        table[a, a] = -np.sum(table[a])
    return table


def node_matrices():
    n = NODE1
    scale = n * (n - 1) / 4.0
    der = lobatto_derivative(n).astype(np.float32).astype(np.float64)
    eye = np.eye(n)
    low, high = np.zeros((n, n)), np.zeros((n, n))
    low[0, 0] = 1.0
    high[n - 1, n - 1] = 1.0
    to_low, to_high = np.zeros((n, n)), np.zeros((n, n))
    to_low[0, n - 1] = 1.0
    to_high[n - 1, 0] = 1.0

    def place(m, d):
        parts = [eye, eye, eye]
        parts[d] = m
        return np.kron(np.kron(parts[0], parts[1]), parts[2])

    own = [place(der + scale * (low - high), d) for d in range(3)]
    own.append(DISSIPATION * scale * sum(place(low + high, d) for d in range(3)))
    for d in range(3):
        own.append(place(scale * (to_high - to_low), d))
        own.append(-DISSIPATION * scale * place(to_high + to_low, d))
    return np.stack(own).astype(np.float32)


def time_weights(count):
    half = count // 2
    d = np.zeros(count)
    for m in range(1, count):
        d[m] = 0.5 * FREQUENCY * (-1.0) ** m / math.tan(math.pi * m / count)
    d[half] = 0.0
    plus = np.zeros((half, half))
    minus = np.zeros((half, half))
    for t in range(half):
        for s in range(half):
            a, b = d[(t - s) % count], d[(t - s + half) % count]
            plus[t, s] = 0.5 * (a + b)
            minus[t, s] = 0.5 * (a - b)
    return plus, minus


def split(x):
    hi = x.astype(BF)
    return hi, (x - hi.astype(F32)).astype(BF)


def mm(a, b):
    return jnp.dot(a, b, preferred_element_type=F32)


def kernel(
    cfg, flux_hbm, nodes_hbm, cross_hbm, match_hbm, state_hbm, forcing_hbm, jac_hbm, res, upd,
    xbuf, ybuf, dbuf, halo, match_up, v1, spat1, part, forc, jac, jone, jtwo, vh, vl, wh, wl, py, pz, pb, pa,
    flux, nodes, cross, match, state, known, send_sem, frecv, brecv, hrecv, mrecv, lsem,
):
    n, ns, T, width, rows, arows, count, cells = cfg
    brows = rows - arows
    block = width * 64
    first = [(p * rows, min(arows, block - p * rows)) for p in range(n) if p * rows < block]
    second = [(p * rows + arows, min(brows, block - p * rows - arows)) for p in range(n) if p * rows + arows < block]
    early = sum(size for _, size in first)
    me = lax.axis_index("inst")
    sp = lax.axis_index("space")
    right, left = lax.rem(sp + 1, ns), lax.rem(sp + ns - 1, ns)
    side, quarter = n // 2, n // 4
    high = jnp.where(me >= side, 1, 0)
    own, other = high * side, (1 - high) * side
    inner, odd = me - own, me % 2
    upper = jnp.where(inner >= quarter, 1, 0)
    spot = inner - upper * quarter
    ranked = [other + lax.rem(k + (1 - high) * quarter, side) for k in range(side)]
    peers = [other + lax.rem(k + odd * (1 - 2 * (k % 2)) + (1 - high) * quarter, side) for k in range(side)]
    peers += [own + (1 - upper) * quarter + lax.rem(spot + k, quarter) for k in range(quarter)]
    peers += [own + upper * quarter + lax.rem(spot + k, quarter) for k in range(1, quarter)]
    lead, held, near = range(quarter), range(quarter, side), range(side, n - 1)
    beside, mates = near[:quarter], near[quarter:]
    middle = high != upper
    turn = [k + (quarter if k < quarter else -quarter) if k < side else k for k in range(n - 1)]

    barrier = pltpu.get_barrier_semaphore()
    for p in (right, left):
        pl.semaphore_signal(barrier, inc=1, device_id={"space": p}, device_id_type=MESH)

    @pl.when(middle)
    def _():
        for k in (*held, *mates, *beside):
            pl.semaphore_signal(barrier, inc=1, device_id={"inst": peers[k]}, device_id_type=MESH)

    def tell(what, who):
        for k in who:
            pl.semaphore_signal(known.at[what], inc=1, device_id={"inst": peers[k]}, device_id_type=MESH)

    pairs = (
        (state_hbm, state), (match_hbm, match), (cross_hbm, cross), (flux_hbm, flux),
        (nodes_hbm, nodes), (forcing_hbm, forc), (jac_hbm, jac),
    )
    loads = [pltpu.make_async_copy(a, b, lsem.at[i % 5]) for i, (a, b) in enumerate(pairs)]
    load_s, load_m, load_c, load_x, load_n, load_f, load_j = loads
    load_s.start()
    load_m.start()
    load_s.wait()
    load_m.wait()
    pl.semaphore_wait(barrier, jnp.where(middle, 2 * quarter - 1, quarter) + 2)

    padded = n * rows != block
    exact0 = state
    if padded:
        for t in range(T):
            v1[0, t, 0:block, :] = state[t]
            v1[0, t, block:, :] = jnp.zeros((n * rows - block, LANES), F32)
            v1[1, t, block:, :] = jnp.zeros((n * rows - block, LANES), F32)
        exact0 = v1.at[0]

    def forward(sweep, src, k, c):
        p = peers[turn[k] if sweep else k]
        if sweep == 0 and c == 0:
            t0, nt, r0, nr = 0, T, 0, arows
        elif c < T:
            t0, nt, r0, nr = c, 1, 0, arows
        else:
            t0, nt, r0, nr = 0, T, arows, brows
        return pltpu.make_async_remote_copy(
            src_ref=src.at[pl.ds(t0, nt), pl.ds(pl.multiple_of(p * rows + r0, 8), nr), :],
            dst_ref=xbuf.at[sweep, pl.ds(me * T + t0, nt), pl.ds(r0, nr), :],
            send_sem=send_sem.at[0],
            recv_sem=frecv.at[c // T],
            device_id={"inst": p},
            device_id_type=MESH,
        )

    def piece(sweep, k, part, t0, nt, sem):
        p = ranked[k] if sweep > 0 and k < side else peers[k]
        r0, nr = ((0, arows), (arows, brows))[part]
        return pltpu.make_async_remote_copy(
            src_ref=ybuf.at[sweep, pl.ds(p * T + t0, nt), pl.ds(r0, nr), :],
            dst_ref=dbuf.at[sweep, pl.ds(t0, nt), pl.ds(pl.multiple_of(me * rows + r0, 8), nr), :],
            send_sem=send_sem.at[1],
            recv_sem=brecv.at[sem],
            device_id={"inst": p},
            device_id_type=MESH,
        )

    def backward(k, c):
        if c < T:
            return piece(0, k, 1, c, 1, c)
        return piece(0, k, 0, 0, T, T)

    def backward_last(k, part, g):
        t0, nt = groups[g]
        return piece(SWEEPS - 1, k, part, t0, nt, 2 * g + part)

    everyone = range(n - 1)
    groups = [(t0, min(2, T - t0)) for t0 in range(0, T, 2)]
    others = pl.ds(0, (n - 1) * T)

    def drain(view, sem):
        pltpu.make_async_copy(view, view, sem).wait()

    def wait_forward(sweep, part):
        at = pl.ds(arows, brows) if part else pl.ds(0, arows)
        drain(xbuf.at[sweep, others, at, :], frecv.at[part])

    def wait_backward(c):
        if c == T:
            drain(dbuf.at[0, :, pl.ds(0, (n - 1) * arows), :], brecv.at[T])
        else:
            drain(dbuf.at[0, c, pl.ds(0, (n - 1) * brows), :], brecv.at[c])

    def wait_last(g, part):
        t0, nt = groups[g]
        size = (n - 1) * (arows, brows)[part]
        drain(dbuf.at[SWEEPS - 1, pl.ds(t0, nt), pl.ds(0, size), :], brecv.at[2 * g + part])

    def halos(sweep, src):
        out = []
        for t in range(T):
            for v in range(width):
                up = v * 64 + 48
                down = v * 64
                out.append(pltpu.make_async_remote_copy(
                    src_ref=src.at[t, pl.ds(up, 16), :],
                    dst_ref=halo.at[sweep, 0, t, pl.ds(v * 16, 16), :],
                    send_sem=send_sem.at[2],
                    recv_sem=hrecv.at[sweep],
                    device_id={"space": right}, device_id_type=MESH))
                out.append(pltpu.make_async_remote_copy(
                    src_ref=src.at[t, pl.ds(down, 16), :],
                    dst_ref=halo.at[sweep, 1, t, pl.ds(v * 16, 16), :],
                    send_sem=send_sem.at[2],
                    recv_sem=hrecv.at[sweep],
                    device_id={"space": left}, device_id_type=MESH))
        return out

    send_match = pltpu.make_async_remote_copy(
        src_ref=match, dst_ref=match_up, send_sem=mrecv.at[0], recv_sem=mrecv.at[1],
        device_id={"space": left}, device_id_type=MESH)

    plus, minus = time_weights(count)
    half = count // 2

    def derive(sweep, first, size):
        def group(g, _):
            at = pl.ds(pl.multiple_of(first + g * 8, 8), 8)
            low = [xbuf[sweep, s, at, :] for s in range(half)]
            high = [xbuf[sweep, s + half, at, :] for s in range(half)]
            sums = [a + b for a, b in zip(low, high)]
            diffs = [a - b for a, b in zip(low, high)]
            for t in range(half):
                acc, dif = None, None
                for s in range(half):
                    if abs(plus[t, s]) > 1e-12:
                        term = sums[s] * float(plus[t, s])
                        acc = term if acc is None else acc + term
                    if abs(minus[t, s]) > 1e-12:
                        term = diffs[s] * float(minus[t, s])
                        dif = term if dif is None else dif + term
                ybuf[sweep, t, at, :] = acc + dif
                ybuf[sweep, t + half, at, :] = acc - dif
            return 0
        lax.fori_loop(0, size // 8, group, 0)

    src_row = lax.broadcasted_iota(jnp.int32, (LANES, LANES), 0)
    dst_col = lax.broadcasted_iota(jnp.int32, (LANES, LANES), 1)

    def onehot(mask):
        return jnp.where(mask, 1.0, 0.0).astype(F32)

    def build_weights():
        lane_var = lax.broadcasted_iota(jnp.int32, (1, block), 1) // 64
        tiles = [jnp.concatenate([nodes[i]] * width, axis=1) for i in range(10)]
        for w in range(width):
            fe = []
            for d in range(3):
                row = jnp.zeros((1, block), F32)
                for v in range(width):
                    row = jnp.where(lane_var == v, flux[w, d:d + 1, v:v + 1], row)
                fe.append(row)
            same = jnp.where(lane_var == w, 1.0, 0.0)
            parts = [fe[0] * tiles[0] + fe[1] * tiles[1] + fe[2] * tiles[2] + same * tiles[3]]
            for d in range(3):
                parts.append(fe[d] * tiles[4 + 2 * d] + same * tiles[5 + 2 * d])
            hi, lo = split(jnp.concatenate(parts, axis=1))
            wh[w * 64:(w + 1) * 64, :] = hi
            wl[w * 64:(w + 1) * 64, :] = lo

    def build_moves():
        layer = (lax.broadcasted_iota(jnp.int32, (1, LANES), 1) // cells) * cells
        for f in range(4):
            nb = cross[f:f + 1, :]
            nb = jnp.concatenate([nb] * (LANES // cells), axis=1) + layer
            ref = py if f < 2 else pz
            ref[(f % 2) * LANES:(f % 2 + 1) * LANES, :] = onehot(src_row == nb).astype(BF)

    def build_match():
        last = LANES - cells
        low_ok = jnp.where(sp > 0, 1.0, 0.0)
        high_ok = jnp.where(sp < ns - 1, 1.0, 0.0)
        shift_up = onehot(dst_col == src_row + cells).astype(BF)
        shift_down = onehot(src_row == dst_col + cells).astype(BF)
        for t in range(T):
            m = jnp.concatenate([match[t]] * (LANES // cells), axis=1)
            mu = jnp.concatenate([match_up[t]] * (LANES // cells), axis=1)
            pb[t, 0:LANES, :] = shift_up
            pb[t, LANES:, :] = (onehot((dst_col < cells) & (src_row == m + last)) * low_ok).astype(BF)
            pa[t, 0:LANES, :] = shift_down
            turned = onehot((dst_col < cells) & (src_row == mu + last)) * high_ok
            pa[t, LANES:, :] = turned.T.astype(BF)

    row_id = lax.broadcasted_iota(jnp.int32, (block, 1), 0)

    def as_mask(index, value):
        return jnp.where(index == value, 1.0, 0.0).astype(F32)

    mj3, mj0 = as_mask((row_id >> 2) & 3, 3), as_mask((row_id >> 2) & 3, 0)
    mk3, mk0 = as_mask(row_id & 3, 3), as_mask(row_id & 3, 0)

    def spread_cross(src, t):
        cols = slice(t * LANES, (t + 1) * LANES)
        x = src[t, 0:block, :]
        for part, out in zip(split(x), (vh, vl)):
            out[0:block, cols] = part
            wide = part.astype(F32)
            y = jnp.concatenate([wide * mj3, wide * mj0], axis=1).astype(BF)
            z = jnp.concatenate([wide * mk3, wide * mk0], axis=1).astype(BF)
            out[2 * block:3 * block, cols] = mm(y, py[...]).astype(BF)
            out[3 * block:4 * block, cols] = mm(z, pz[...]).astype(BF)

    def spread_flow(sweep, src, t):
        cols = slice(t * LANES, (t + 1) * LANES)
        own_high = jnp.concatenate([src[t, v * 64 + 48:v * 64 + 64, :] for v in range(width)], axis=0)
        own_low = jnp.concatenate([src[t, v * 64:v * 64 + 16, :] for v in range(width)], axis=0)
        high = split(jnp.concatenate([own_high, halo[sweep, 0, t]], axis=1))
        low = split(jnp.concatenate([own_low, halo[sweep, 1, t]], axis=1))
        for i, out in enumerate((vh, vl)):
            ub = mm(high[i], pb[t]).astype(BF)
            ua = mm(low[i], pa[t]).astype(BF)
            for v in range(width):
                base = block + v * 64
                out[base:base + 16, cols] = ua[v * 16:(v + 1) * 16]
                out[base + 48:base + 64, cols] = ub[v * 16:(v + 1) * 16]

    def clear_middle():
        for out in (vh, vl):
            for v in range(width):
                base = block + v * 64 + 16
                out[base:base + 32, :] = jnp.zeros((32, T * LANES), BF)

    def split_jac():
        load_j.wait()
        place = lax.broadcasted_iota(jnp.int32, (block, block), 0)
        column = lax.broadcasted_iota(jnp.int32, (block, block), 1)
        chosen, at = column < 0, 0
        for start, size in first + second:
            chosen = chosen | ((column >= at) & (column < at + size) & (place - column == start - at))
            at += size
        chosen = onehot(chosen).astype(BF)
        for t in range(T):
            hi, lo = [mm(part, chosen).astype(BF) for part in split(jac[t])]
            jone[t] = jnp.concatenate([hi[:, :early], lo[:, :early], hi[:, :early]], axis=1)
            jtwo[t] = jnp.concatenate([hi[:, early:], lo[:, early:], hi[:, early:]], axis=1)

    def apply_space(spat):
        total = mm(wh[...], vh[...]) + mm(wl[...], vh[...]) + mm(wh[...], vl[...])
        for t in range(T):
            spat[t] = total[:, t * LANES:(t + 1) * LANES] - forc[t]

    def start_early(sweep):
        if sweep == 0:
            for k in everyone:
                backward(k, T).start()
            return
        for g in range(len(groups)):
            for k in (*lead, *near):
                backward_last(k, 0, g).start()

    def start_late(sweep):
        if sweep == 0:
            for c in range(T):
                for k in everyone:
                    backward(k, c).start()
            return
        for g in range(len(groups)):
            for k in lead:
                backward_last(k, 1, g).start()
        for g in range(len(groups)):
            for k in near:
                backward_last(k, 1, g).start()
        for k in held:
            for g in range(len(groups)):
                for part in range(2):
                    backward_last(k, part, g).start()

    own_rows = pl.ds(pl.multiple_of(me * rows, 8), rows)
    own_times = pl.ds(me * T, T)

    def run_sweep(sweep, src, before, between):
        xbuf[sweep, own_times, :, :] = src[:, own_rows, :]
        for job in before:
            job()
        wait_forward(sweep, 0)
        derive(sweep, 0, arows)
        start_early(sweep)
        for job in between:
            job()
        wait_forward(sweep, 1)
        derive(sweep, arows, brows)
        start_late(sweep)
        dbuf[sweep, :, own_rows, :] = ybuf[sweep, own_times, :, :]

    def step(sweep, spat, t, spans, weights):
        r = []
        for start, size in spans:
            at = slice(start, start + size)
            r.append(spat[t, at, :] + dbuf[sweep, t, at, :])
            if sweep == 0:
                spat[t, at, :] = r[-1]
        hi, lo = split(jnp.concatenate(r, axis=0))
        return mm(weights[t], jnp.concatenate([hi, hi, lo], axis=0))

    def finish(src, spat, dst, after):
        wait_backward(T)
        for t in range(T):
            part[t] = src[t, 0:block, :] - step(0, spat, t, first, jone)
        for t in range(T):
            wait_backward(t)
            dst[t, 0:block, :] = part[t] - step(0, spat, t, second, jtwo)
            after(t)

    def finish_last(src, spat, dst):
        for g, (t0, nt) in enumerate(groups):
            wait_last(g, 0)
            for t in range(t0, t0 + nt):
                part[t] = src[t, 0:block, :] - step(1, spat, t, first, jone)
            wait_last(g, 1)
            for t in range(t0, t0 + nt):
                dst[t, 0:block, :] = part[t] - step(1, spat, t, second, jtwo)

    def send_forward(sweep, src, c):
        for k in everyone:
            forward(sweep, src, k, c).start()

    def wait_halos(sweep, src):
        drain(halo.at[sweep], hrecv.at[sweep])

    def first_halo_ready():
        send_match.wait()
        wait_halos(0, state)
        build_match()

    def send_first(who):
        for c in (0, T):
            for k in who:
                forward(0, exact0, k, c).start()

    @pl.when(middle)
    def _():
        send_first((*held, *mates))
        pl.semaphore_wait(known.at[0], quarter)
        tell(1, held)
        pl.semaphore_wait(known.at[1], quarter)
        tell(2, beside)
        send_first((*lead, *beside))

    @pl.when(jnp.logical_not(middle))
    def _():
        tell(0, beside)
        send_first(beside)
        pl.semaphore_wait(known.at[2], quarter)
        send_first((*lead, *held, *mates))

    for load in loads[2:]:
        load.start()
    send_match.start()
    for h in halos(0, state):
        h.start()
    before = [load_c.wait, build_moves, load_n.wait, load_x.wait, build_weights]
    before += [functools.partial(spread_cross, state, t) for t in range(T)]
    before += [clear_middle]
    between = [first_halo_ready]
    between += [functools.partial(spread_flow, 0, state, t) for t in range(T)]
    between += [load_f.wait, functools.partial(apply_space, res), split_jac]
    run_sweep(0, exact0, before, between)
    cur = v1.at[1]
    finish(state, res, cur, lambda t: send_forward(1, cur, t))

    send_forward(1, cur, T)
    for h in halos(1, cur):
        h.start()
    before = [functools.partial(spread_cross, cur, t) for t in range(T)]
    between = [functools.partial(wait_halos, 1, cur)]
    between += [functools.partial(spread_flow, 1, cur, t) for t in range(T)]
    between += [functools.partial(apply_space, spat1)]
    run_sweep(1, cur, before, between)
    finish_last(cur, spat1, upd)
    drain(xbuf.at[:, others, :, :], send_sem.at[0])
    drain(ybuf.at[:, others, :, :], send_sem.at[1])
    drain(halo, send_sem.at[2])


def hand_out(res_vmem, upd_vmem, res_hbm, upd_hbm, sem):
    copies = [
        pltpu.make_async_copy(res_vmem, res_hbm, sem.at[0]),
        pltpu.make_async_copy(upd_vmem, upd_hbm, sem.at[1]),
    ]
    for copy in copies:
        copy.start()
    for copy in copies:
        copy.wait()


def body(n, ns, state, forcing, flux_jac, jacobi_inv, cross_nbr, lower_match):
    T, block, elements = state.shape
    width = flux_jac.shape[1]
    cells = cross_nbr.shape[1]
    count = n * T
    rows = -(-block // (8 * n)) * 8
    arows = -(-rows // 16) * 8
    halo_rows = width * 16
    early = sum(max(0, min(arows, block - p * rows)) for p in range(n))
    flux = flux_jac.transpose(1, 0, 2)
    nodes = jnp.asarray(node_matrices())
    cfg = (n, ns, T, width, rows, arows, count, cells)
    full = n * rows
    dma = pltpu.SemaphoreType.DMA
    vmem = pl.BlockSpec(memory_space=pltpu.VMEM)
    hbm = pl.BlockSpec(memory_space=pl.ANY)
    held = pltpu.VMEM(state.shape, F32)
    res, upd = pl.pallas_call(
        functools.partial(kernel, cfg),
        name="sweeps",
        out_shape=(held, held),
        in_specs=[hbm] * 7,
        out_specs=(vmem, vmem),
        scratch_shapes=[
            pltpu.VMEM((SWEEPS, count, rows, LANES), F32),
            pltpu.VMEM((SWEEPS, count, rows, LANES), F32),
            pltpu.VMEM((SWEEPS, T, full, LANES), F32),
            pltpu.VMEM((SWEEPS, 2, T, halo_rows, LANES), F32),
            pltpu.VMEM((T, 1, cells), jnp.int32),
            pltpu.VMEM((2, T, full, LANES), F32),
            pltpu.VMEM((T, block, LANES), F32),
            pltpu.VMEM((T, block, LANES), F32),
            pltpu.VMEM((T, block, LANES), F32),
            pltpu.VMEM((T, block, block), F32),
            pltpu.VMEM((T, block, 3 * early), BF),
            pltpu.VMEM((T, block, 3 * (block - early)), BF),
            pltpu.VMEM((4 * block, T * LANES), BF),
            pltpu.VMEM((4 * block, T * LANES), BF),
            pltpu.VMEM((block, 4 * block), BF),
            pltpu.VMEM((block, 4 * block), BF),
            pltpu.VMEM((2 * LANES, LANES), BF),
            pltpu.VMEM((2 * LANES, LANES), BF),
            pltpu.VMEM((T, 2 * LANES, LANES), BF),
            pltpu.VMEM((T, 2 * LANES, LANES), BF),
            pltpu.VMEM(flux.shape, F32),
            pltpu.VMEM(nodes.shape, F32),
            pltpu.VMEM(cross_nbr.shape, jnp.int32),
            pltpu.VMEM(lower_match.shape, jnp.int32),
            pltpu.VMEM((T, block, LANES), F32),
            pltpu.SemaphoreType.REGULAR((3,)),
            dma((3,)),
            dma((2,)),
            dma((T + 1,)),
            dma((SWEEPS,)),
            dma((2,)),
            dma((5,)),
        ],
        compiler_params=pltpu.CompilerParams(
            collective_id=0, has_side_effects=True, vmem_limit_bytes=56 * 1024 * 1024
        ),
    )(flux, nodes, cross_nbr, lower_match, state, forcing, jacobi_inv)
    out = jax.ShapeDtypeStruct(state.shape, F32)
    return pl.pallas_call(
        hand_out,
        name="hand_out",
        out_shape=(out, out),
        in_specs=[vmem] * 2,
        out_specs=(hbm, hbm),
        scratch_shapes=[dma((2,))],
    )(pltpu.with_memory_space_constraint(res, pltpu.VMEM), pltpu.with_memory_space_constraint(upd, pltpu.VMEM))


def solution(mesh):
    n, ns = mesh.shape["inst"], mesh.shape["space"]
    return jax.shard_map(
        functools.partial(body, n, ns),
        mesh=mesh,
        in_specs=(
            P("inst", None, "space"),
            P("inst", None, "space"),
            P(),
            P("inst", None, None),
            P(),
            P("inst", "space", None),
        ),
        out_specs=(P("inst", None, "space"), P("inst", None, "space")),
        check_vma=False,
    )
```
